128 devices in a mesh: lat: 16 (over y, z), lon: 8 (over x, core).
Axes of the slice: x: 4, y: 4, z: 4, core: 2. Of those that a mesh axis runs over, the one named last changes fastest.
Arguments:
- control: float32 [512, 256, 512], P('lat', 'lon'), may hold values from -6 to 6
- vertical_half: bfloat16 [512, 512], replicated, may hold values from -0.25 to 0.25
- error_scale: bfloat16 [512, 256, 512], P('lat', 'lon'), may hold values from 0.29882812 to 3
- jacobian: bfloat16 [128, 2048, 512], P(('lat', 'lon')), may hold values from -0.25 to 0.25
- inverse_r: float32 [4, 128, 128], replicated, may hold values from -1 to 3, as said below
- channel_mask: int32 [128, 16, 128], P(('lat', 'lon')), may hold values 0 or 1
- group_instrument: int32 [128, 16], P(('lat', 'lon')), may hold values from 0 to 3
- outbound_columns: int32 [128, 2048], P(('lat', 'lon')), may hold values from 0 to 1023
- observation_row: int32 [128, 16, 256], P(('lat', 'lon')), may hold values from 0 to 2047
Outputs:
- hessian_product: float32 [512, 256, 512], P('lat', 'lon')
The draws below stay inside these ranges and needn't reach their ends.
Inputs may be any that keep to these rules, and one draw needn't show every extreme that they name: `outbound_columns`: entry p * 16 + s of device q's row is the local column that q sends to device p in place s. `observation_row`: row q * 16 + s of what a device receives is the column that device q sent to it in place s. `inverse_r`: each instrument's block is symmetric.
All inputs are finite; a program needn't handle non-finite values. No bound on the sum of `channel_mask` on one device may be relied on, other than what follows from the above.
Results may differ from the reference program's by a relative error of at most 0.013.
Values may be sent and summed in bfloat16 or wider, within the bound.
No kernel may reach another device: no remote copies, remote signals or barrier semaphores. Data moves between devices by JAX's collectives and lax.ppermute only.
A program may use at most 128 MiB of HBM per device.

```python
import math
import jax
import jax.numpy as jnp
from jax import lax

TILE_LAT_ROWS = 32
TILE_LON_COLUMNS = 32
CH = 128
NINST = 4
SLOT = 16
DEVICE_GROUPS = 16
GROUP_OBSERVES = 256
K = 512
NLAT = 512
NLON = 256
RECEIVED_COLUMNS = 2048
N_LAT = 16
N_LON = 8
DEVICES = 128


def draw_inverse_r(key, part):
    first, second = jax.random.split(jax.random.fold_in(key, 11))
    diagonal = jnp.exp(jax.random.uniform(first, (NINST, CH), jnp.float32, -0.69, 0.69))
    noise = jax.random.normal(second, (NINST, CH, CH), jnp.float32) * (0.6 / CH ** 0.5)
    noise = jnp.clip(noise, -0.9, 0.9)
    symmetric = 0.5 * (noise + jnp.swapaxes(noise, 1, 2))
    identity = jnp.eye(CH, dtype=jnp.float32)[None]
    return (symmetric * (1.0 - identity) + identity * diagonal[:, None, :]).astype(jnp.float32)


def set_ends(result, key, smallest, top_value):
    spot = [jax.random.randint(jax.random.fold_in(key, axis), (), 0, length) for axis, length in enumerate(result.shape)]
    main_axis = result.shape.index(max(result.shape))
    next_to = spot[:main_axis] + [(spot[main_axis] + 1) % result.shape[main_axis]] + spot[main_axis + 1:]
    return result.at[tuple(spot)].set(smallest).at[tuple(next_to)].set(top_value)


def block_scale(rng, shape, shards, smallest, top_value):
    level, own = 1.0, jax.random.fold_in(rng, 6)
    for axis_at, parts in shards:
        heights = jnp.exp(jax.random.uniform(jax.random.fold_in(own, axis_at), (parts,), jnp.float32, smallest / len(shards), top_value / len(shards)))
        level = level * jnp.repeat(heights, shape[axis_at] // parts).reshape([-1 if axis == axis_at else 1 for axis in range(len(shape))])
    return level


def scatter_about(key, extent, spread, most, cuts=(), kind=jnp.bfloat16):
    values = jax.random.normal(key, extent, jnp.float32) * spread
    if len(cuts) > 0:
        values = block_scale(key, extent, cuts, -0.22, 0.18) * values
    return jnp.clip(values, min=-most, max=most).astype(kind)


def setup_inputs(seed: int = 0) -> dict:
    arg_keys = jax.random.split(jax.random.key(seed), 10)
    return {
        "control": scatter_about(arg_keys[0], (NLAT, NLON, K), 1.0, 6.0, ((0, 16), (1, 8)), jnp.float32),
        "vertical_half": scatter_about(arg_keys[1], (K, K), K ** -0.5, 0.25),
        "error_scale": jnp.clip(jnp.exp(math.log(3.0) - 2.306499 * jax.random.uniform(arg_keys[2], (NLAT, NLON, K), jnp.float32) ** block_scale(arg_keys[2], (NLAT, NLON, K), ((0, 16), (1, 8)), -0.2, 0.2)), 0.29882812, 3.0).astype(jnp.bfloat16),
        "jacobian": scatter_about(arg_keys[3], (DEVICES, DEVICE_GROUPS * CH, K), K ** -0.5, 0.25, ((0, 128),)),
        "inverse_r": draw_inverse_r(jax.random.fold_in(arg_keys[9], 71), 0),
        "channel_mask": set_ends((jax.random.randint(arg_keys[5], (DEVICES, DEVICE_GROUPS, CH), 0, 4) < 3).astype(jnp.int32), jax.random.fold_in(arg_keys[5], 1), 0, 1),
        "group_instrument": set_ends(jax.random.randint(arg_keys[6], (DEVICES, DEVICE_GROUPS), 0, NINST), jax.random.fold_in(arg_keys[6], 1), 0, NINST - 1).astype(jnp.int32),
        "outbound_columns": set_ends(jax.random.randint(arg_keys[7], (DEVICES, RECEIVED_COLUMNS), 0, TILE_LAT_ROWS * TILE_LON_COLUMNS), jax.random.fold_in(arg_keys[7], 1), 0, (TILE_LAT_ROWS * TILE_LON_COLUMNS) - 1).astype(jnp.int32),
        "observation_row": set_ends(jax.random.randint(arg_keys[8], (DEVICES, DEVICE_GROUPS, GROUP_OBSERVES), 0, RECEIVED_COLUMNS), jax.random.fold_in(arg_keys[8], 1), 0, RECEIVED_COLUMNS - 1).astype(jnp.int32),
    }


diffusion = 0.2


def relax(field):
    padded = jnp.pad(field, ((1, 1), (0, 0), (0, 0)))
    west = jnp.roll(field, 1, axis=1)
    east = jnp.roll(field, -1, axis=1)
    return field + diffusion * (padded[:-2] + padded[2:] + west + east - 4.0 * field)


def observe(predicted_values, slots, used, selected):
    group_list, column_count = slots.shape
    channel_list = used.shape[1]
    received_count = predicted_values.shape[0]
    lookup_table = predicted_values.reshape(received_count, group_list, channel_list)
    group_ids = jnp.arange(group_list).astype(jnp.int32)[:, None]
    picked = lookup_table[slots, group_ids]
    usedf = used.astype(jnp.float32)[:, None, :]
    model_obs = picked * usedf
    weighted_residual = jnp.einsum("gce,goe->goc", selected, model_obs, precision=lax.Precision.HIGHEST) * usedf
    column_index = (slots * group_list + group_ids).astype(jnp.int32).reshape(-1)
    summed_values = jax.ops.segment_sum(weighted_residual.reshape(group_list * column_count, channel_list), column_index, received_count * group_list)
    return summed_values.reshape(received_count, group_list * channel_list).astype(jnp.bfloat16)


def reference(control, vertical_half, error_scale, jacobian, inverse_r, channel_mask, group_instrument, outbound_columns, observation_row):
    column_count = NLAT * NLON
    control_bf = control.astype(jnp.bfloat16).reshape(column_count, K)
    vertical = jnp.dot(control_bf, vertical_half.T, preferred_element_type=jnp.float32).reshape(NLAT, NLON, K)
    scale = error_scale.astype(jnp.float32)
    state = (scale * relax(relax(vertical))).astype(jnp.bfloat16).reshape(column_count, K)
    devices = N_LAT * N_LON
    source = jnp.arange(devices).astype(jnp.int32)
    lists = outbound_columns.reshape(devices, devices, SLOT).astype(jnp.int32)
    lat_block = (source // N_LON)[:, None, None]
    lon_block = (source % N_LON)[:, None, None]
    global_col = (lat_block * TILE_LAT_ROWS + lists // TILE_LON_COLUMNS) * NLON + lon_block * TILE_LON_COLUMNS + lists % TILE_LON_COLUMNS
    columns_for = jnp.transpose(global_col, (1, 0, 2)).reshape(devices, devices * SLOT).astype(jnp.int32)

    def visit(total, inputs):
        columns, jac, slots, used, instrument = inputs
        received = state[columns].astype(jnp.float32)
        jac_full = jac.astype(jnp.float32)
        predicted_values = jnp.dot(received, jac_full.T, precision=lax.Precision.HIGHEST)
        selected = inverse_r[instrument]
        collected = observe(predicted_values, slots, used, selected)
        slot_adjoint = jnp.dot(collected.astype(jnp.float32), jac_full, precision=lax.Precision.HIGHEST)
        rounded = lax.optimization_barrier(slot_adjoint.astype(jnp.bfloat16))
        return total.at[columns].add(rounded.astype(jnp.float32)), None

    total, unused = lax.scan(visit, jnp.zeros((column_count, K), jnp.float32), (columns_for, jacobian, observation_row, channel_mask, group_instrument))
    back = relax(relax(scale * total.reshape(NLAT, NLON, K))).astype(jnp.bfloat16).reshape(column_count, K)
    return control + jnp.dot(back, vertical_half, preferred_element_type=jnp.float32).reshape(NLAT, NLON, K)
```

```python
import functools

import jax
import jax.numpy as jnp
from jax import lax
from jax.experimental import pallas as pl
from jax.experimental.pallas import tpu as pltpu
from jax.sharding import PartitionSpec as P

diffusion = 0.2


def from_before(cells, axis, wrap):
    count = lax.axis_size(axis)
    return lax.ppermute(cells, axis, [(i, (i + 1) % count) for i in range(count if wrap else count - 1)])


def from_after(cells, axis, wrap):
    count = lax.axis_size(axis)
    return lax.ppermute(cells, axis, [((i + 1) % count, i) for i in range(count if wrap else count - 1)])


def borders(cells):
    above = from_before(cells[-2:], "lat", False)
    below = from_after(cells[:2], "lat", False)

    def taller(columns):
        return jnp.concatenate([above[1:, columns], cells[:, columns], below[:1, columns]], axis=0)

    west = from_before(taller(slice(-2, None)), "lon", True)
    east = from_after(taller(slice(0, 2)), "lon", True)
    return above, below, west, east


def relax(padded):
    center = padded[1:-1, 1:-1]
    return center + diffusion * (
        padded[:-2, 1:-1] + padded[2:, 1:-1] + padded[1:-1, :-2] + padded[1:-1, 2:] - 4.0 * center
    )


def smooth_twice(cells, above, below, west, east):
    tall = jnp.concatenate([above, cells, below], axis=0)
    sides = [jnp.pad(side, ((1, 1), (0, 0), (0, 0))) for side in (west, east)]
    once = relax(jnp.concatenate([sides[0], tall, sides[1]], axis=1))
    rows = once.shape[0]
    position = jnp.arange(rows)
    band = lax.axis_index("lat")
    outside = (position < 1) & (band == 0) | (position >= rows - 1) & (band == lax.axis_size("lat") - 1)
    return relax(jnp.where(outside[:, None, None], 0.0, once))


def observe_kernel(
    instrument, received, jacobian, inverse_r, used, slots, adjoint, weights, collected
):
    f32, bf16 = jnp.float32, jnp.bfloat16
    rows, width = received.shape
    groups, _, channels = used.shape
    observes = slots.shape[2]
    half = rows // 2
    for n in range(inverse_r.shape[0]):
        whole = inverse_r[n]
        high = whole.astype(bf16)
        low = (whole - high.astype(f32)).astype(bf16)
        both = jnp.concatenate([high, low], axis=1)
        weights[n] = jnp.concatenate([both, both], axis=0)

    def group(g, table):
        slot = slots[g]
        lanes = jnp.broadcast_to(slot, (channels, observes)).T
        upper = lanes >= half
        local = jnp.where(upper, lanes - half, lanes)
        lane = lax.broadcasted_iota(jnp.int32, (observes, channels), 1)
        picker = jnp.concatenate(
            [jnp.where(local == lane + t * channels, 1.0, 0.0).astype(bf16) for t in range(half // channels)],
            axis=1,
        )
        found = jnp.dot(picker, table, preferred_element_type=f32)
        mask = used[g].astype(f32)
        model = jnp.where(upper, found[:, channels:], found[:, :channels]) * mask
        high = model.astype(bf16)
        low = (model - high.astype(f32)).astype(bf16)
        parts = jnp.dot(
            jnp.concatenate([high, low], axis=1), weights[instrument[g]], preferred_element_type=f32
        )
        weighted = (parts[:, :channels] + parts[:, channels:]) * mask
        split = jnp.concatenate(
            [jnp.where(upper, 0.0, weighted), jnp.where(upper, weighted, 0.0)], axis=1
        ).astype(bf16)
        position = lax.broadcasted_iota(jnp.int32, (half, observes), 0)
        slot_local = jnp.where(slot >= half, slot - half, slot)
        placer = jnp.where(position == slot_local, 1.0, 0.0).astype(bf16)
        return jnp.dot(placer, split, preferred_element_type=f32).astype(bf16)

    @pl.loop(0, groups // 2)
    def _(p):
        block = jacobian[pl.ds(pl.multiple_of(p * 2 * channels, 2 * channels), 2 * channels), :]
        predicted = lax.dot_general(
            received[...], block, (((1,), (1,)), ((), ())), preferred_element_type=f32
        ).astype(bf16)
        sums = []
        for i in range(2):
            columns = slice(i * channels, (i + 1) * channels)
            table = jnp.concatenate([predicted[:half, columns], predicted[half:, columns]], axis=1)
            sums.append(group(2 * p + i, table))
        collected[p, :half] = jnp.concatenate([s[:, :channels] for s in sums], axis=1)
        collected[p, half:] = jnp.concatenate([s[:, channels:] for s in sums], axis=1)

    step = 512

    @pl.loop(0, rows // step)
    def _(b):
        at = pl.ds(pl.multiple_of(b * step, step), step)
        total = jnp.zeros((step, width), f32)
        for p in range(groups // 2):
            total += jnp.dot(
                collected[p, at],
                jacobian[p * 2 * channels : (p + 1) * 2 * channels, :],
                preferred_element_type=f32,
            )
        adjoint[at, :] = total.astype(bf16)


def observe(received, weights, inverse_r, used, instrument, slots):
    rows, width = received.shape
    groups, channels = used.shape
    vmem = pl.BlockSpec(memory_space=pltpu.VMEM)
    pairs = groups // 2
    flops = 4 * rows * width * groups * channels + 4 * slots.size * rows * channels
    return pl.pallas_call(
        observe_kernel,
        out_shape=jax.ShapeDtypeStruct((rows, width), jnp.bfloat16),
        in_specs=[pl.BlockSpec(memory_space=pltpu.SMEM)] + [vmem] * 5,
        out_specs=vmem,
        scratch_shapes=[
            pltpu.VMEM((inverse_r.shape[0], 2 * channels, 2 * channels), jnp.bfloat16),
            pltpu.VMEM((pairs, rows, 2 * channels), jnp.bfloat16),
        ],
        cost_estimate=pl.CostEstimate(
            flops=flops, bytes_accessed=6 * rows * width, transcendentals=0
        ),
        compiler_params=pltpu.CompilerParams(vmem_limit_bytes=48 * 1024 * 1024),
    )(
        instrument,
        received,
        weights,
        inverse_r,
        used.reshape(groups, 1, channels),
        slots.reshape(groups, 1, slots.shape[1]),
    )


def on_device(
    control,
    vertical_half,
    error_scale,
    jacobian,
    inverse_r,
    channel_mask,
    group_instrument,
    outbound_columns,
    observation_row,
):
    f32, bf16 = jnp.float32, jnp.bfloat16
    lat_rows, lon_cols, width = control.shape
    cells = lat_rows * lon_cols
    devices = lax.axis_size("lat") * lax.axis_size("lon")
    lists = outbound_columns.reshape(-1)
    places = lists.shape[0] // devices
    scale = error_scale.astype(f32)

    def exchange(columns):
        return lax.all_to_all(
            columns.reshape(devices, places, width),
            ("lat", "lon"),
            split_axis=0,
            concat_axis=0,
            tiled=True,
        ).reshape(devices * places, width)

    def lift(part):
        flat = part.reshape(-1, width)
        return jnp.dot(flat, vertical_half.T, preferred_element_type=f32).reshape(part.shape)

    control_bf = control.astype(bf16)
    parts = (control_bf, *borders(control_bf))
    state = (scale * smooth_twice(*[lift(part) for part in parts])).astype(bf16).reshape(cells, width)
    picker = (lists[:, None] == jnp.arange(cells)[None, :]).astype(bf16)
    outgoing = jnp.dot(picker, state, preferred_element_type=f32).astype(bf16)
    slot_adjoint = observe(
        exchange(outgoing),
        jacobian[0],
        inverse_r,
        channel_mask[0],
        group_instrument[0],
        observation_row[0],
    )
    column_adjoint = jnp.dot(picker.T, exchange(slot_adjoint), preferred_element_type=f32)
    scaled = scale * column_adjoint.reshape(lat_rows, lon_cols, width)
    around = [part.astype(f32) for part in borders(scaled.astype(bf16))]
    back = smooth_twice(scaled, *around).astype(bf16)
    result = jnp.dot(back.reshape(cells, width), vertical_half, preferred_element_type=f32)
    return control + result.reshape(lat_rows, lon_cols, width)


def solution(mesh):
    placed = (
        P("lat", "lon", None),
        P(),
        P("lat", "lon", None),
        P(("lat", "lon"), None, None),
        P(),
        P(("lat", "lon"), None, None),
        P(("lat", "lon"), None),
        P(("lat", "lon"), None),
        P(("lat", "lon"), None, None),
    )
    return jax.shard_map(
        on_device, mesh=mesh, in_specs=placed, out_specs=P("lat", "lon", None), check_vma=False
    )
```

```python
import jax
import jax.numpy as jnp
from jax import lax
from jax.experimental import pallas as pl
from jax.experimental.pallas import tpu as pltpu
from jax.sharding import PartitionSpec as P

f32, bf16 = jnp.float32, jnp.bfloat16
weight_twice = 0.04
lanes_wide = 128
around = 48
parts = 4
limit = 48 * 1024 * 1024
VMEM = pl.BlockSpec(memory_space=pltpu.VMEM)
SMEM = pl.BlockSpec(memory_space=pltpu.SMEM)
HBM = pl.BlockSpec(memory_space=pltpu.HBM)


def from_before(cells, axis, wrap):
    count = lax.axis_size(axis)
    return lax.ppermute(cells, axis, [(i, (i + 1) % count) for i in range(count if wrap else count - 1)])


def from_after(cells, axis, wrap):
    count = lax.axis_size(axis)
    return lax.ppermute(cells, axis, [((i + 1) % count, i) for i in range(count if wrap else count - 1)])


def exchange_borders(top, bottom, left, right):
    above = from_before(bottom, "lat", False)
    below = from_after(top, "lat", False)

    def taller(columns, at):
        column, rows, width = columns.shape
        under = jnp.swapaxes(below[:1, at], 0, 1)
        over = jnp.swapaxes(above[1:, at], 0, 1)
        gap = jnp.zeros((column, around - rows - 2, width), columns.dtype)
        return jnp.concatenate([columns, under, gap, over], axis=1)

    west = from_before(taller(right, slice(-2, None)), "lon", True)
    east = from_after(taller(left, slice(0, 2)), "lon", True)
    return above, below, west, east


def inside_poles():
    band = lax.axis_index("lat")
    ends = jnp.stack([band != 0, band != lax.axis_size("lat") - 1])
    return ends.astype(f32)


def sum_twice(center, above, below, west, east, inside, at, emit):
    rows, cols = center.shape[0], center.shape[1]
    ring = cols + 8
    sublane = lax.broadcasted_iota(jnp.int32, (8, lanes_wide), 0)

    def side(i):
        if not -1 <= i <= rows:
            return jnp.zeros((8, lanes_wide), f32)
        place = around - 1 if i < 0 else i
        e0, e1, w0, w1 = [
            jnp.broadcast_to(half[n, pl.ds(place, 1), at], (8, lanes_wide))
            for half in (east, west)
            for n in range(2)
        ]
        return jnp.where(sublane < 1, e0, jnp.where(sublane < 2, e1, jnp.where(sublane < 7, w0, w1)))

    def line(i):
        if i < 0:
            own = above[i + 2, :, at]
        elif i < rows:
            own = center[i, :, at]
        else:
            own = below[i - rows, :, at]
        return jnp.concatenate([own, side(i)], axis=0)

    def total(before, here, after):
        return (here + before) + (after + (pltpu.roll(here, 1, 0) + pltpu.roll(here, ring - 1, 0)))

    lines = [line(-2), line(-1)]
    sums = []
    for i in range(-1, rows + 1):
        lines.append(line(i + 1))
        once = total(*lines)
        lines.pop(0)
        if i < 0:
            once = once * inside[0]
        if i == rows:
            once = once * inside[1]
        sums.append(once)
        if len(sums) == 3:
            emit(i - 1, total(*sums)[:cols])
            sums.pop(0)


def lift_kernel(control, scale, vertical_half, vertical, held_scale, left, right, held, sems):
    rows, cols, width = held.shape
    high = rows // parts

    def get(b):
        place = pl.ds(pl.multiple_of(b * high, high), high)
        return pltpu.make_async_copy(control.at[place], held.at[place], sems.at[b])

    keep = pltpu.make_async_copy(scale, held_scale, sems.at[parts])
    for b in range(parts):
        get(b).start()
    keep.start()

    @pl.loop(0, parts)
    def _(b):
        get(b).wait()
        place = pl.ds(pl.multiple_of(b * high, high), high)
        cells = held[place].astype(bf16)
        vertical[place] = lax.dot_general(
            cells.reshape(high * cols, width),
            vertical_half[...],
            (((1,), (1,)), ((), ())),
            preferred_element_type=f32,
        ).reshape(high, cols, width)

    for n in range(2):
        left[n] = held[:, n, :].astype(bf16)
        right[n] = held[:, cols - 2 + n, :].astype(bf16)
    keep.wait()


def lift(control, scale, vertical_half):
    rows, cols, width = control.shape
    side = jax.ShapeDtypeStruct((2, rows, width), bf16)
    return pl.pallas_call(
        lift_kernel,
        out_shape=(
            jax.ShapeDtypeStruct(control.shape, f32),
            jax.ShapeDtypeStruct(scale.shape, scale.dtype),
            side,
            side,
        ),
        in_specs=[HBM, HBM, VMEM],
        out_specs=(VMEM,) * 4,
        scratch_shapes=[pltpu.VMEM(control.shape, f32), pltpu.SemaphoreType.DMA((parts + 1,))],
        cost_estimate=pl.CostEstimate(
            flops=2 * rows * cols * width * width, bytes_accessed=6 * rows * cols * width, transcendentals=0
        ),
        compiler_params=pltpu.CompilerParams(vmem_limit_bytes=limit),
    )(control, scale, vertical_half)


def pick_kernel(
    inside, center, above, below, west, east, vertical_half, scale, lists, outgoing, lines, sides, state
):
    rows, cols, width = center.shape

    def lift(cells):
        return lax.dot_general(
            cells, vertical_half[...], (((1,), (1,)), ((), ())), preferred_element_type=f32
        )

    for n, border in enumerate((above, below)):
        lines[n] = lift(border[...].reshape(-1, width)).reshape(border.shape)
    for n, border in enumerate((west, east)):
        sides[n] = lift(border[...].reshape(-1, width)).reshape(border.shape)

    @pl.loop(0, width // lanes_wide)
    def _(c):
        at = pl.ds(pl.multiple_of(c * lanes_wide, lanes_wide), lanes_wide)

        def emit(i, values):
            own = scale[i, :, at].astype(f32) * weight_twice
            state[i * cols : (i + 1) * cols, at] = (own * values).astype(bf16)

        sum_twice(center, lines.at[0], lines.at[1], sides.at[0], sides.at[1], inside, at, emit)

    cells = rows * cols
    count = lists.shape[2]
    lane = lax.broadcasted_iota(jnp.int32, (count, lanes_wide), 1)

    @pl.loop(0, parts)
    def _(b):
        wanted = jnp.broadcast_to(lists[b], (lanes_wide, count)).T
        picker = jnp.concatenate(
            [jnp.where(wanted - t == lane, 1.0, 0.0).astype(bf16) for t in range(0, cells, lanes_wide)],
            axis=1,
        )
        place = pl.ds(pl.multiple_of(b * count, count), count)
        outgoing[place, :] = jnp.dot(picker, state[...], preferred_element_type=f32).astype(bf16)


def pick(inside, center, borders, vertical_half, scale, lists):
    rows, cols, width = center.shape
    slots = lists.size
    return pl.pallas_call(
        pick_kernel,
        out_shape=jax.ShapeDtypeStruct((slots, width), bf16),
        in_specs=[SMEM] + [VMEM] * 8,
        out_specs=VMEM,
        scratch_shapes=[
            pltpu.VMEM((2, 2, cols, width), f32),
            pltpu.VMEM((2, 2, around, width), f32),
            pltpu.VMEM((rows * cols, width), bf16),
        ],
        cost_estimate=pl.CostEstimate(
            flops=2 * slots * rows * cols * width, bytes_accessed=4 * slots * width, transcendentals=0
        ),
        compiler_params=pltpu.CompilerParams(vmem_limit_bytes=limit),
    )(inside, center, *borders, vertical_half, scale, lists)


def observe_kernel(
    instrument,
    jacobian,
    inverse_r,
    used,
    slots,
    received,
    adjoint,
    weights,
    table,
    collected,
):
    rows, width = received.shape
    _, groups, channels = used.shape
    observes = slots.shape[2]
    half = rows // 2
    step = rows // parts
    together = 4

    def block(b):
        return pl.ds(pl.multiple_of(b * step, step), step)

    for n in range(inverse_r.shape[0]):
        whole = inverse_r[n]
        high = whole.astype(bf16)
        low = (whole - high.astype(f32)).astype(bf16)
        both = jnp.concatenate([high, low], axis=1)
        weights[n] = jnp.concatenate([both, both], axis=0)

    @pl.loop(0, parts // 2)
    def _(b):
        for p in range(groups // 2):
            pair = jacobian[p * 2 * channels : (p + 1) * 2 * channels, :]
            for n in range(2):
                predicted = lax.dot_general(
                    received[block(b + n * (parts // 2)), :],
                    pair,
                    (((1,), (1,)), ((), ())),
                    preferred_element_type=f32,
                ).astype(bf16)
                for i in range(2):
                    table[2 * p + i, block(b), n * channels : (n + 1) * channels] = predicted[
                        :, i * channels : (i + 1) * channels
                    ]

    lane = lax.broadcasted_iota(jnp.int32, (observes, channels), 1)
    position = lax.broadcasted_iota(jnp.int32, (half, observes), 0)

    def group(g):
        slot = slots[0, pl.ds(g, 1), :]
        wanted = jnp.broadcast_to(slot, (channels, observes)).T
        upper = wanted >= half
        local = jnp.where(upper, wanted - half, wanted)
        picker = jnp.concatenate(
            [jnp.where(local - t == lane, 1.0, 0.0).astype(bf16) for t in range(0, half, channels)],
            axis=1,
        )
        found = jnp.dot(picker, table[g], preferred_element_type=f32)
        mask = used[0, pl.ds(g, 1), :].astype(f32)
        model = jnp.where(upper, found[:, channels:], found[:, :channels]) * mask
        high = model.astype(bf16)
        low = (model - high.astype(f32)).astype(bf16)
        products = jnp.dot(
            jnp.concatenate([high, low], axis=1), weights[instrument[g]], preferred_element_type=f32
        )
        weighted = (products[:, :channels] + products[:, channels:]) * mask
        split = jnp.concatenate(
            [jnp.where(upper, 0.0, weighted), jnp.where(upper, weighted, 0.0)], axis=1
        ).astype(bf16)
        placer = jnp.where(position == jnp.where(slot >= half, slot - half, slot), 1.0, 0.0).astype(bf16)
        return jnp.dot(placer, split, preferred_element_type=f32).astype(bf16)

    @pl.loop(0, groups // together)
    def _(q):
        sums = [group(q * together + i) for i in range(together)]
        for i, both in enumerate(sums):
            p, columns = q * (together // 2) + i // 2, slice(i % 2 * channels, (i % 2 + 1) * channels)
            collected[p, :half, columns] = both[:, :channels]
            collected[p, half:, columns] = both[:, channels:]

    @pl.loop(0, parts)
    def _(b):
        total = jnp.zeros((step, width), f32)
        for p in range(groups // 2):
            total += jnp.dot(
                collected[p, block(b)],
                jacobian[p * 2 * channels : (p + 1) * 2 * channels, :],
                preferred_element_type=f32,
            )
        adjoint[block(b), :] = total.astype(bf16)


def observe(received, weights, inverse_r, used, instrument, slots):
    rows, width = received.shape
    _, groups, channels = used.shape
    flops = 4 * rows * width * groups * channels + 4 * slots.size * rows * channels
    return pl.pallas_call(
        observe_kernel,
        out_shape=jax.ShapeDtypeStruct((rows, width), bf16),
        in_specs=[SMEM] + [VMEM] * 5,
        out_specs=VMEM,
        scratch_shapes=[
            pltpu.VMEM((inverse_r.shape[0], 2 * channels, 2 * channels), bf16),
            pltpu.VMEM((groups, rows // 2, 2 * channels), bf16),
            pltpu.VMEM((groups // 2, rows, 2 * channels), bf16),
        ],
        cost_estimate=pl.CostEstimate(flops=flops, bytes_accessed=6 * rows * width, transcendentals=0),
        compiler_params=pltpu.CompilerParams(vmem_limit_bytes=limit),
    )(
        instrument,
        weights,
        inverse_r,
        used,
        slots,
        received,
    )


def gather_kernel(scale, lists, returned, scaled, top, bottom, left, right):
    rows, cols, width = scaled.shape
    count = lists.shape[2]
    high = rows // 4
    step = high * cols

    cell = lax.broadcasted_iota(jnp.int32, (step, count), 0)

    @pl.loop(0, rows // high)
    def _(m):
        total = jnp.zeros((step, width), f32)
        for b in range(parts):
            placer = jnp.where(cell == lists[b] - m * step, 1.0, 0.0).astype(bf16)
            total += jnp.dot(placer, returned[b * count : (b + 1) * count, :], preferred_element_type=f32)
        at = pl.ds(m * high, high)
        scaled[at] = total.reshape(high, cols, width) * scale[at].astype(f32)

    top[...] = scaled[:2].astype(bf16)
    bottom[...] = scaled[rows - 2 :].astype(bf16)
    for n in range(2):
        left[n] = scaled[:, n, :].astype(bf16)
        right[n] = scaled[:, cols - 2 + n, :].astype(bf16)


def gather(scale, lists, returned):
    rows, cols, width = scale.shape
    slots = lists.size
    border = jax.ShapeDtypeStruct((2, cols, width), bf16)
    side = jax.ShapeDtypeStruct((2, rows, width), bf16)
    return pl.pallas_call(
        gather_kernel,
        out_shape=(jax.ShapeDtypeStruct(scale.shape, f32), border, border, side, side),
        in_specs=[VMEM] * 3,
        out_specs=(VMEM,) * 5,
        cost_estimate=pl.CostEstimate(
            flops=2 * slots * rows * cols * width, bytes_accessed=4 * slots * width, transcendentals=0
        ),
        compiler_params=pltpu.CompilerParams(vmem_limit_bytes=limit),
    )(scale, lists, returned)


def finish_kernel(
    inside, center, above, below, west, east, vertical_half, control, product, lines, sides, back, summed, sems
):
    rows, cols, width = center.shape
    for n, border in enumerate((above, below)):
        lines[n] = border[...].astype(f32)
    for n, border in enumerate((west, east)):
        sides[n] = border[...].astype(f32)

    @pl.loop(0, width // lanes_wide)
    def _(c):
        at = pl.ds(pl.multiple_of(c * lanes_wide, lanes_wide), lanes_wide)

        def emit(i, values):
            back[i * cols : (i + 1) * cols, at] = (weight_twice * values).astype(bf16)

        sum_twice(center, lines.at[0], lines.at[1], sides.at[0], sides.at[1], inside, at, emit)

    high = rows // parts

    def put(b):
        place = pl.ds(b * high, high)
        return pltpu.make_async_copy(summed.at[place], product.at[place], sems.at[b])

    @pl.loop(0, parts)
    def _(b):
        place = pl.ds(pl.multiple_of(b * high * cols, high * cols), high * cols)
        result = jnp.dot(back[place, :], vertical_half[...], preferred_element_type=f32)
        at = pl.ds(b * high, high)
        summed[at] = control[at] + result.reshape(high, cols, width)
        put(b).start()

    for b in range(parts):
        put(b).wait()


def finish(inside, center, borders, vertical_half, control):
    rows, cols, width = center.shape
    return pl.pallas_call(
        finish_kernel,
        out_shape=jax.ShapeDtypeStruct(control.shape, f32),
        in_specs=[SMEM] + [VMEM] * 7,
        out_specs=HBM,
        scratch_shapes=[
            pltpu.VMEM((2, 2, cols, width), f32),
            pltpu.VMEM((2, 2, around, width), f32),
            pltpu.VMEM((rows * cols, width), bf16),
            pltpu.VMEM(control.shape, f32),
            pltpu.SemaphoreType.DMA((parts,)),
        ],
        cost_estimate=pl.CostEstimate(
            flops=2 * rows * cols * width * width, bytes_accessed=12 * rows * cols * width, transcendentals=0
        ),
        compiler_params=pltpu.CompilerParams(vmem_limit_bytes=limit),
    )(inside, center, *borders, vertical_half, control)


def on_device(
    control,
    vertical_half,
    error_scale,
    jacobian,
    inverse_r,
    channel_mask,
    group_instrument,
    outbound_columns,
    observation_row,
):
    rows, cols, width = control.shape
    devices = lax.axis_size("lat") * lax.axis_size("lon")
    slots = outbound_columns.size
    lists = outbound_columns.reshape(parts, 1, slots // parts)
    inside = inside_poles()

    def exchange(columns):
        return lax.all_to_all(
            columns.reshape(devices, slots // devices, width),
            ("lat", "lon"),
            split_axis=0,
            concat_axis=0,
            tiled=True,
        ).reshape(slots, width)

    vertical, scale, left, right = lift(control, error_scale, vertical_half)
    ends = lax.optimization_barrier((control[:2], control[-2:]))
    borders = exchange_borders(*[end.astype(bf16) for end in ends], left, right)
    outgoing = pick(inside, vertical, borders, vertical_half, scale, lists)
    slot_adjoint = observe(
        exchange(outgoing),
        jacobian[0],
        inverse_r,
        channel_mask,
        group_instrument[0],
        observation_row,
    )
    scaled, top, bottom, left, right = gather(scale, lists, exchange(slot_adjoint))
    return finish(inside, scaled, exchange_borders(top, bottom, left, right), vertical_half, control)


def solution(mesh):
    placed = (
        P("lat", "lon", None),
        P(),
        P("lat", "lon", None),
        P(("lat", "lon"), None, None),
        P(),
        P(("lat", "lon"), None, None),
        P(("lat", "lon"), None),
        P(("lat", "lon"), None),
        P(("lat", "lon"), None, None),
    )
    return jax.shard_map(
        on_device, mesh=mesh, in_specs=placed, out_specs=P("lat", "lon", None), check_vma=False
    )
```

```python
import jax
import jax.numpy as jnp
from jax import lax
from jax.experimental import pallas as pl
from jax.experimental.pallas import tpu as pltpu
from jax.sharding import PartitionSpec as P

f32, bf16 = jnp.float32, jnp.bfloat16
weight_twice = 0.04
lanes_wide = 128
around = 48
parts = 4
mebi = 1024 * 1024
VMEM = pl.BlockSpec(memory_space=pltpu.VMEM)
SMEM = pl.BlockSpec(memory_space=pltpu.SMEM)
HBM = pl.BlockSpec(memory_space=pltpu.HBM)


def from_before(cells, axis):
    count = lax.axis_size(axis)
    return lax.ppermute(cells, axis, [(i, (i + 1) % count) for i in range(count)])


def from_after(cells, axis):
    count = lax.axis_size(axis)
    return lax.ppermute(cells, axis, [((i + 1) % count, i) for i in range(count)])


def exchange_borders(top, bottom, left, right, held):
    above = from_before(bottom, "lat")
    below = from_after(top, "lat")

    def taller(columns, at):
        column, rows, width = columns.shape
        under = jnp.swapaxes(below[:1, at], 0, 1)
        over = jnp.swapaxes(above[1:, at], 0, 1)
        gap = jnp.zeros((column, around - rows - 2, width), columns.dtype)
        return jnp.concatenate([columns, under, gap, over], axis=1)

    to_east, to_west, held = lax.optimization_barrier(
        (taller(right, slice(-2, None)), taller(left, slice(0, 2)), held)
    )
    west = from_before(to_east, "lon")
    east = from_after(to_west, "lon")
    return (above, below, west, east), held


def inside_poles():
    band = lax.axis_index("lat")
    ends = jnp.stack([band != 0, band != lax.axis_size("lat") - 1])
    return ends.astype(f32)


def stay(array):
    return pltpu.with_memory_space_constraint(array, pltpu.HBM)


def neighbours(before, here, after):
    ring = here.shape[0]
    return (here + before) + (after + (pltpu.roll(here, 1, 0) + pltpu.roll(here, ring - 1, 0)))


def lane_blocks(width):
    def run(body):
        @pl.loop(0, width // lanes_wide)
        def _(c):
            body(pl.ds(pl.multiple_of(c * lanes_wide, lanes_wide), lanes_wide))

    return run


def sum_twice_inside(center, at, emit):
    rows = center.shape[0]
    lines, sums = [center[0, :, at], center[1, :, at]], []
    for i in range(1, rows - 1):
        lines.append(center[i + 1, :, at])
        sums.append(neighbours(*lines))
        lines.pop(0)
        if len(sums) == 3:
            emit(i - 1, neighbours(*sums))
            sums.pop(0)


def sum_twice_edges(center, left, right, lines, sides, inside, at, emit):
    above, below = lines.at[0], lines.at[1]
    west, east = sides.at[0], sides.at[1]
    rows = center.shape[0]
    sublane = lax.broadcasted_iota(jnp.int32, (8, lanes_wide), 0)
    keep = jnp.where(sublane == 7, inside[0], jnp.where(sublane == 0, inside[1], 1.0))

    def cell(line, n, place):
        return jnp.broadcast_to(line[n, pl.ds(place, 1), at], (8, lanes_wide))

    def ends(e0, e1, w0, w1):
        return jnp.where(sublane < 1, e0, jnp.where(sublane < 2, e1, jnp.where(sublane < 7, w0, w1)))

    def row_line(own, i):
        if not -1 <= i <= rows:
            return jnp.concatenate([own, jnp.zeros((8, lanes_wide), f32)], axis=0)
        place = around - 1 if i < 0 else i
        tail = ends(cell(east, 0, place), cell(east, 1, place), cell(west, 0, place), cell(west, 1, place))
        if not 0 <= i < rows:
            tail = tail * inside[0 if i < 0 else 1]
        return jnp.concatenate([own, tail], axis=0)

    def column_line(own, j):
        tail = ends(cell(below, 0, j), cell(below, 1, j), cell(above, 0, j), cell(above, 1, j))
        return jnp.concatenate([own, tail], axis=0)

    def outer_column(side, n):
        after, before = cell(side, n, rows) * inside[1], cell(side, n, around - 1) * inside[0]
        return jnp.concatenate([side[n, :rows, at], ends(after, after, before, before)], axis=0)

    last = rows - 1
    edges = (
        [row_line(above[n, :, at], n - 2) for n in range(2)] + [row_line(center[n, :, at], n) for n in range(4)],
        [row_line(below[1 - n, :, at], rows + 1 - n) for n in range(2)]
        + [row_line(center[last - n, :, at], last - n) for n in range(4)],
        [outer_column(west, n) for n in range(2)] + [column_line(left[n, :, at], n) for n in range(4)],
        [outer_column(east, 1 - n) for n in range(2)]
        + [column_line(right[3 - n, :, at], last - n) for n in range(4)],
    )
    for e, edge in enumerate(edges):
        sums = [neighbours(*edge[n : n + 3]) for n in range(4)]
        if e < 2:
            sums[0] = sums[0] * inside[e]
        else:
            sums = [jnp.concatenate([s[:rows], s[rows:] * keep], axis=0) for s in sums]
        for n in range(2):
            emit(e, n, neighbours(*sums[n : n + 3])[:rows])


def edge_number(cell, rows, cols):
    row, col = cell // cols, cell % cols
    number = jnp.where(col < 2, 4 * cols + col * rows + row, -1)
    number = jnp.where(col >= cols - 2, 4 * cols + (2 + cols - 1 - col) * rows + row, number)
    number = jnp.where(row < 2, row * cols + col, number)
    return jnp.where(row >= rows - 2, (2 + rows - 1 - row) * cols + col, number)


def edge_lines(cells):
    rows, cols = cells.shape[0], cells.shape[1]
    return (
        [cells[0], cells[1], cells[rows - 1], cells[rows - 2]]
        + [cells[:, n, :] for n in (0, 1)]
        + [cells[:, cols - 1 - n, :] for n in (0, 1)]
    )


def borders_kernel(control, top, bottom, left, right, ends, flanks, sems):
    rows, cols, _ = control.shape
    copies = [
        pltpu.make_async_copy(control.at[pl.ds(0, 2)], ends.at[0], sems.at[0]),
        pltpu.make_async_copy(control.at[pl.ds(rows - 2, 2)], ends.at[1], sems.at[1]),
        pltpu.make_async_copy(control.at[:, pl.ds(0, 8)], flanks.at[0], sems.at[2]),
        pltpu.make_async_copy(control.at[:, pl.ds(cols - 8, 8)], flanks.at[1], sems.at[3]),
    ]
    for copy in copies:
        copy.start()
    for n, out in enumerate((top, bottom)):
        copies[n].wait()
        out[...] = ends[n].astype(bf16)
    for n, out in enumerate((left, right)):
        copies[2 + n].wait()
        for i in range(2):
            out[i] = flanks[n, :, 6 * n + i, :].astype(bf16)


def own_borders(control):
    rows, cols, width = control.shape
    side = jax.ShapeDtypeStruct((2, rows, width), bf16)
    border = jax.ShapeDtypeStruct((2, cols, width), bf16)
    return pl.pallas_call(
        borders_kernel,
        out_shape=(border, border, side, side),
        in_specs=[HBM],
        out_specs=(VMEM,) * 4,
        scratch_shapes=[
            pltpu.VMEM((2, 2, cols, width), f32),
            pltpu.VMEM((2, rows, 8, width), f32),
            pltpu.SemaphoreType.DMA((4,)),
        ],
        cost_estimate=pl.CostEstimate(flops=0, bytes_accessed=80 * rows * width, transcendentals=0),
        compiler_params=pltpu.CompilerParams(vmem_limit_bytes=8 * mebi),
    )(stay(control))


def lift_kernel(
    control,
    scale,
    vertical_half,
    vertical,
    left,
    right,
    held_scale,
    edge_scale,
    edge_control,
    held,
    weights,
    sems,
):
    rows, cols, width = held.shape
    high = rows // parts

    def get(b):
        place = pl.ds(pl.multiple_of(b * high, high), high)
        return pltpu.make_async_copy(control.at[place], held.at[place], sems.at[b])

    factor = pltpu.make_async_copy(vertical_half, weights, sems.at[parts])
    keep = pltpu.make_async_copy(scale, held_scale, sems.at[parts + 1])
    factor.start()
    for b in range(parts):
        get(b).start()
    keep.start()
    factor.wait()

    @pl.loop(0, parts)
    def _(b):
        get(b).wait()
        place = pl.ds(pl.multiple_of(b * high, high), high)
        cells = held[place].astype(bf16)
        vertical[place] = lax.dot_general(
            cells.reshape(high * cols, width),
            weights[...],
            (((1,), (1,)), ((), ())),
            preferred_element_type=f32,
        ).reshape(high, cols, width)

    for n in range(4):
        left[n] = vertical[:, n, :]
        right[n] = vertical[:, cols - 4 + n, :]
    for n, line in enumerate(edge_lines(held)):
        edge_control[n] = line
    keep.wait()
    for n, line in enumerate(edge_lines(held_scale)):
        edge_scale[n] = line


def lift(control, scale, vertical_half):
    rows, cols, width = control.shape
    side = jax.ShapeDtypeStruct((4, rows, width), f32)
    return pl.pallas_call(
        lift_kernel,
        out_shape=(
            jax.ShapeDtypeStruct(control.shape, f32),
            side,
            side,
            jax.ShapeDtypeStruct(scale.shape, scale.dtype),
            jax.ShapeDtypeStruct((8, rows, width), scale.dtype),
            jax.ShapeDtypeStruct((8, rows, width), f32),
        ),
        in_specs=[HBM] * 3,
        out_specs=(VMEM,) * 6,
        scratch_shapes=[
            pltpu.VMEM(control.shape, f32),
            pltpu.VMEM(vertical_half.shape, bf16),
            pltpu.SemaphoreType.DMA((parts + 2,)),
        ],
        cost_estimate=pl.CostEstimate(
            flops=2 * rows * cols * width * width, bytes_accessed=6 * rows * cols * width, transcendentals=0
        ),
        compiler_params=pltpu.CompilerParams(vmem_limit_bytes=16 * mebi),
    )(stay(control), stay(scale), stay(vertical_half))


def pick_inside_kernel(center, scale, lists, outgoing, state):
    rows, cols, width = center.shape
    for i in (0, 1, rows - 2, rows - 1):
        state[i * cols : (i + 1) * cols] = jnp.zeros((cols, width), bf16)

    @lane_blocks(width)
    def _(at):
        def emit(i, values):
            own = scale[i, :, at].astype(f32) * weight_twice
            state[i * cols : (i + 1) * cols, at] = (own * values).astype(bf16)

        sum_twice_inside(center, at, emit)

    cells = rows * cols
    count = lists.shape[2]
    lane = lax.broadcasted_iota(jnp.int32, (count, lanes_wide), 1)

    @pl.loop(0, parts)
    def _(b):
        cell = lists[b]
        inner = jnp.where(edge_number(cell, rows, cols) < 0, cell, -1)
        wanted = jnp.broadcast_to(inner, (lanes_wide, count)).T
        picker = jnp.concatenate(
            [jnp.where(wanted - t == lane, 1.0, 0.0).astype(bf16) for t in range(0, cells, lanes_wide)],
            axis=1,
        )
        place = pl.ds(pl.multiple_of(b * count, count), count)
        outgoing[place, :] = jnp.dot(picker, state[...], preferred_element_type=f32).astype(bf16)


def pick_inside(center, scale, lists):
    rows, cols, width = center.shape
    slots = lists.size
    return pl.pallas_call(
        pick_inside_kernel,
        out_shape=jax.ShapeDtypeStruct((slots, width), bf16),
        in_specs=[VMEM] * 3,
        out_specs=VMEM,
        scratch_shapes=[pltpu.VMEM((rows * cols, width), bf16)],
        cost_estimate=pl.CostEstimate(
            flops=2 * slots * rows * cols * width, bytes_accessed=4 * slots * width, transcendentals=0
        ),
        compiler_params=pltpu.CompilerParams(vmem_limit_bytes=16 * mebi),
    )(center, scale, lists)


def pick_edges_kernel(
    inside,
    center,
    left,
    right,
    above,
    below,
    west,
    east,
    vertical_half,
    edge_scale,
    lists,
    inner,
    outgoing,
    lines,
    sides,
    state,
):
    rows, cols, width = center.shape

    borders = [border[...].reshape(-1, width) for border in (above, below, west, east)]
    lifted = lax.dot_general(
        jnp.concatenate(borders, axis=0),
        vertical_half[...],
        (((1,), (1,)), ((), ())),
        preferred_element_type=f32,
    )
    start = 0
    for n, border in enumerate((above, below, west, east)):
        part = lifted[start : start + 2 * border.shape[1]].reshape(border.shape)
        start += 2 * border.shape[1]
        if n < 2:
            lines[n] = part * inside[n]
        else:
            sides[n - 2] = part

    @lane_blocks(width)
    def _(at):
        def emit(e, n, values):
            place = 2 * e + n
            own = edge_scale[place, :, at].astype(f32) * weight_twice
            state[place * rows : (place + 1) * rows, at] = (own * values).astype(bf16)

        sum_twice_edges(center, left, right, lines, sides, inside, at, emit)

    count = lists.shape[2]
    edges = state.shape[0]
    lane = lax.broadcasted_iota(jnp.int32, (count, lanes_wide), 1)

    @pl.loop(0, parts)
    def _(b):
        number = edge_number(lists[b], rows, cols)
        wanted = jnp.broadcast_to(number, (lanes_wide, count)).T
        picker = jnp.concatenate(
            [jnp.where(wanted - t == lane, 1.0, 0.0).astype(bf16) for t in range(0, edges, lanes_wide)],
            axis=1,
        )
        place = pl.ds(pl.multiple_of(b * count, count), count)
        edge = jnp.dot(picker, state[...], preferred_element_type=f32)
        outgoing[place, :] = (inner[place, :].astype(f32) + edge).astype(bf16)


def pick_edges(inside, center, left, right, borders, vertical_half, edge_scale, lists, inner):
    rows, cols, width = center.shape
    slots = lists.size
    edges = 8 * rows
    return pl.pallas_call(
        pick_edges_kernel,
        out_shape=jax.ShapeDtypeStruct((slots, width), bf16),
        in_specs=[SMEM] + [VMEM] * 11,
        out_specs=VMEM,
        scratch_shapes=[
            pltpu.VMEM((2, 2, cols, width), f32),
            pltpu.VMEM((2, 2, around, width), f32),
            pltpu.VMEM((edges, width), bf16),
        ],
        cost_estimate=pl.CostEstimate(
            flops=2 * slots * edges * width, bytes_accessed=4 * slots * width, transcendentals=0
        ),
        compiler_params=pltpu.CompilerParams(vmem_limit_bytes=16 * mebi),
    )(inside, center, left, right, *borders, vertical_half, edge_scale, lists, inner)


def observe_kernel(
    instrument,
    jacobian,
    inverse_r,
    used,
    slots,
    received,
    adjoint,
    weights,
    table,
    collected,
):
    rows, width = received.shape
    _, groups, channels = used.shape
    observes = slots.shape[2]
    half = rows // 2
    step = rows // parts
    together = 4

    def block(b):
        return pl.ds(pl.multiple_of(b * step, step), step)

    for n in range(inverse_r.shape[0]):
        whole = inverse_r[n]
        high = whole.astype(bf16)
        low = (whole - high.astype(f32)).astype(bf16)
        both = jnp.concatenate([high, low], axis=1)
        weights[n] = jnp.concatenate([both, both], axis=0)

    @pl.loop(0, parts // 2)
    def _(b):
        for p in range(groups // 2):
            pair = jacobian[p * 2 * channels : (p + 1) * 2 * channels, :]
            for n in range(2):
                predicted = lax.dot_general(
                    received[block(b + n * (parts // 2)), :],
                    pair,
                    (((1,), (1,)), ((), ())),
                    preferred_element_type=f32,
                ).astype(bf16)
                for i in range(2):
                    table[2 * p + i, block(b), n * channels : (n + 1) * channels] = predicted[
                        :, i * channels : (i + 1) * channels
                    ]

    lane = lax.broadcasted_iota(jnp.int32, (observes, channels), 1)
    position = lax.broadcasted_iota(jnp.int32, (half, observes), 0)

    def group(g):
        slot = slots[0, pl.ds(g, 1), :]
        wanted = jnp.broadcast_to(slot, (channels, observes)).T
        upper = wanted >= half
        local = jnp.where(upper, wanted - half, wanted)
        picker = jnp.concatenate(
            [jnp.where(local - t == lane, 1.0, 0.0).astype(bf16) for t in range(0, half, channels)],
            axis=1,
        )
        found = jnp.dot(picker, table[g], preferred_element_type=f32)
        mask = used[0, pl.ds(g, 1), :].astype(f32)
        model = jnp.where(upper, found[:, channels:], found[:, :channels]) * mask
        high = model.astype(bf16)
        low = (model - high.astype(f32)).astype(bf16)
        products = jnp.dot(
            jnp.concatenate([high, low], axis=1), weights[instrument[g]], preferred_element_type=f32
        )
        weighted = (products[:, :channels] + products[:, channels:]) * mask
        split = jnp.concatenate(
            [jnp.where(upper, 0.0, weighted), jnp.where(upper, weighted, 0.0)], axis=1
        ).astype(bf16)
        placer = jnp.where(position == jnp.where(slot >= half, slot - half, slot), 1.0, 0.0).astype(bf16)
        return jnp.dot(placer, split, preferred_element_type=f32).astype(bf16)

    @pl.loop(0, groups // together)
    def _(q):
        sums = [group(q * together + i) for i in range(together)]
        for i, both in enumerate(sums):
            p, columns = q * (together // 2) + i // 2, slice(i % 2 * channels, (i % 2 + 1) * channels)
            collected[p, :half, columns] = both[:, :channels]
            collected[p, half:, columns] = both[:, channels:]

    @pl.loop(0, parts)
    def _(b):
        total = jnp.zeros((step, width), f32)
        for p in range(groups // 2):
            total += jnp.dot(
                collected[p, block(b)],
                jacobian[p * 2 * channels : (p + 1) * 2 * channels, :],
                preferred_element_type=f32,
            )
        adjoint[block(b), :] = total.astype(bf16)


def observe(received, weights, inverse_r, used, instrument, slots):
    rows, width = received.shape
    _, groups, channels = used.shape
    flops = 4 * rows * width * groups * channels + 4 * slots.size * rows * channels
    return pl.pallas_call(
        observe_kernel,
        out_shape=jax.ShapeDtypeStruct((rows, width), bf16),
        in_specs=[SMEM] + [VMEM] * 5,
        out_specs=VMEM,
        scratch_shapes=[
            pltpu.VMEM((inverse_r.shape[0], 2 * channels, 2 * channels), bf16),
            pltpu.VMEM((groups, rows // 2, 2 * channels), bf16),
            pltpu.VMEM((groups // 2, rows, 2 * channels), bf16),
        ],
        cost_estimate=pl.CostEstimate(flops=flops, bytes_accessed=6 * rows * width, transcendentals=0),
        compiler_params=pltpu.CompilerParams(vmem_limit_bytes=40 * mebi),
    )(
        instrument,
        weights,
        inverse_r,
        used,
        slots,
        received,
    )


def gather_edges_kernel(edge_scale, lists, returned, top, bottom, left, right):
    lines, rows, width = edge_scale.shape
    count = lists.shape[2]
    edges = lines * rows
    number = lax.broadcasted_iota(jnp.int32, (edges, count), 0)
    line, position = number // rows, number % rows
    depth = jnp.where(line % 4 < 2, line % 4, rows + 1 - line % 4)
    cell = jnp.where(line < 4, depth * rows + position, position * rows + depth)
    total = jnp.zeros((edges, width), f32)
    for b in range(parts):
        placer = jnp.where(cell == lists[b], 1.0, 0.0).astype(bf16)
        total += jnp.dot(placer, returned[b * count : (b + 1) * count, :], preferred_element_type=f32)
    scaled = (total.reshape(lines, rows, width) * edge_scale[...].astype(f32)).astype(bf16)
    for n in range(2):
        top[n] = scaled[n]
        bottom[1 - n] = scaled[2 + n]
        left[n] = scaled[4 + n]
        right[1 - n] = scaled[6 + n]


def gather_edges(edge_scale, lists, returned):
    lines, rows, width = edge_scale.shape
    slots = lists.size
    border = jax.ShapeDtypeStruct((2, rows, width), bf16)
    return pl.pallas_call(
        gather_edges_kernel,
        out_shape=(border,) * 4,
        in_specs=[VMEM] * 3,
        out_specs=(VMEM,) * 4,
        cost_estimate=pl.CostEstimate(
            flops=2 * slots * lines * rows * width, bytes_accessed=2 * slots * width, transcendentals=0
        ),
        compiler_params=pltpu.CompilerParams(vmem_limit_bytes=16 * mebi),
    )(edge_scale, lists, returned)


def gather_kernel(scale, lists, returned, scaled, left, right):
    rows, cols, width = scaled.shape
    count = lists.shape[2]
    high = rows // parts
    step = high * cols
    cell = lax.broadcasted_iota(jnp.int32, (step, count), 0)

    @pl.loop(0, parts)
    def _(m):
        total = jnp.zeros((step, width), f32)
        for b in range(parts):
            placer = jnp.where(cell == lists[b] - m * step, 1.0, 0.0).astype(bf16)
            total += jnp.dot(placer, returned[b * count : (b + 1) * count, :], preferred_element_type=f32)
        at = pl.ds(m * high, high)
        scaled[at] = total.reshape(high, cols, width) * scale[at].astype(f32)

    for n in range(4):
        left[n] = scaled[:, n, :]
        right[n] = scaled[:, cols - 4 + n, :]


def gather(scale, lists, returned):
    rows, cols, width = scale.shape
    slots = lists.size
    side = jax.ShapeDtypeStruct((4, rows, width), f32)
    return pl.pallas_call(
        gather_kernel,
        out_shape=(jax.ShapeDtypeStruct(scale.shape, f32), side, side),
        in_specs=[VMEM] * 3,
        out_specs=(VMEM,) * 3,
        cost_estimate=pl.CostEstimate(
            flops=slots * rows * cols * width // 2, bytes_accessed=slots * width, transcendentals=0
        ),
        compiler_params=pltpu.CompilerParams(vmem_limit_bytes=16 * mebi),
    )(scale, lists, returned)


def finish_inside_kernel(center, vertical_half, control, product, back):
    rows, cols, width = center.shape
    for i in (0, 1, rows - 2, rows - 1):
        back[i * cols : (i + 1) * cols] = jnp.zeros((cols, width), bf16)

    @lane_blocks(width)
    def _(at):
        def emit(i, values):
            back[i * cols : (i + 1) * cols, at] = (weight_twice * values).astype(bf16)

        sum_twice_inside(center, at, emit)

    high = rows // parts

    @pl.loop(0, parts)
    def _(b):
        place = pl.ds(pl.multiple_of(b * high * cols, high * cols), high * cols)
        result = jnp.dot(back[place, :], vertical_half[...], preferred_element_type=f32)
        at = pl.ds(b * high, high)
        product[at] = control[at] + result.reshape(high, cols, width)


def finish_inside(center, vertical_half, control):
    rows, cols, width = center.shape
    return pl.pallas_call(
        finish_inside_kernel,
        out_shape=jax.ShapeDtypeStruct(control.shape, f32),
        in_specs=[VMEM] * 3,
        out_specs=VMEM,
        scratch_shapes=[pltpu.VMEM((rows * cols, width), bf16)],
        cost_estimate=pl.CostEstimate(
            flops=2 * rows * cols * width * width, bytes_accessed=8 * rows * cols * width, transcendentals=0
        ),
        compiler_params=pltpu.CompilerParams(vmem_limit_bytes=16 * mebi),
    )(center, vertical_half, control)


def finish_edges_kernel(
    inside,
    center,
    left,
    right,
    above,
    below,
    west,
    east,
    vertical_half,
    edge_control,
    inner,
    product,
    lines,
    sides,
    back,
    ends,
    flanks,
    sems,
):
    rows, cols, width = center.shape
    body = pl.ds(2, rows - 4)

    def put(source, place, n):
        copy = pltpu.make_async_copy(source, product.at[place], sems.at[n])
        copy.start()
        return copy

    copies = [put(inner.at[body, pl.ds(8, cols - 16)], (body, pl.ds(8, cols - 16)), 0)]
    for n, border in enumerate((above, below)):
        lines[n] = border[...].astype(f32) * inside[n]
    for n, border in enumerate((west, east)):
        sides[n] = border[...].astype(f32)

    @lane_blocks(width)
    def _(at):
        def emit(e, n, values):
            place = 2 * e + n
            back[place * rows : (place + 1) * rows, at] = (weight_twice * values).astype(bf16)

        sum_twice_edges(center, left, right, lines, sides, inside, at, emit)

    result = jnp.dot(back[...], vertical_half[...], preferred_element_type=f32)
    edge = edge_control[...] + result.reshape(edge_control.shape)
    for n in range(2):
        ends[0, n] = edge[n]
        ends[1, 1 - n] = edge[2 + n]
    copies.append(put(ends.at[0], pl.ds(0, 2), 1))
    copies.append(put(ends.at[1], pl.ds(rows - 2, 2), 2))
    sublane = lax.broadcasted_iota(jnp.int32, (8, width), 0)
    for side in range(2):
        start = side * (cols - 8)
        for i in range(2, rows - 2):
            block = inner[i, start : start + 8, :]
            for n in range(2):
                outer = jnp.broadcast_to(edge[4 + 2 * side + n, i : i + 1, :], (8, width))
                block = jnp.where(sublane == (n if side == 0 else 7 - n), outer, block)
            flanks[side, i - 2] = block
        copies.append(put(flanks.at[side], (body, pl.ds(start, 8)), 3 + side))
    for copy in copies:
        copy.wait()


def finish_edges(inside, center, left, right, borders, vertical_half, edge_control, inner):
    rows, cols, width = center.shape
    return pl.pallas_call(
        finish_edges_kernel,
        out_shape=jax.ShapeDtypeStruct(inner.shape, f32),
        in_specs=[SMEM] + [VMEM] * 10,
        out_specs=HBM,
        scratch_shapes=[
            pltpu.VMEM((2, 2, cols, width), f32),
            pltpu.VMEM((2, 2, around, width), f32),
            pltpu.VMEM((8 * rows, width), bf16),
            pltpu.VMEM((2, 2, cols, width), f32),
            pltpu.VMEM((2, rows - 4, 8, width), f32),
            pltpu.SemaphoreType.DMA((5,)),
        ],
        cost_estimate=pl.CostEstimate(
            flops=16 * rows * width * width, bytes_accessed=4 * rows * cols * width, transcendentals=0
        ),
        compiler_params=pltpu.CompilerParams(vmem_limit_bytes=16 * mebi),
    )(inside, center, left, right, *borders, vertical_half, edge_control, inner)


def on_device(
    control,
    vertical_half,
    error_scale,
    jacobian,
    inverse_r,
    channel_mask,
    group_instrument,
    outbound_columns,
    observation_row,
):
    rows, cols, width = control.shape
    devices = lax.axis_size("lat") * lax.axis_size("lon")
    slots = outbound_columns.size
    lists = outbound_columns.reshape(parts, 1, slots // parts)
    inside = inside_poles()

    def exchange(columns):
        return lax.all_to_all(
            columns.reshape(devices, slots // devices, width),
            ("lat", "lon"),
            split_axis=0,
            concat_axis=0,
            tiled=True,
        ).reshape(slots, width)

    own = own_borders(control)
    vertical, left, right, scale, edge_scale, edge_control = lift(control, error_scale, vertical_half)
    borders, held = exchange_borders(*own, vertical)
    inner = pick_inside(held, scale, lists)
    outgoing = pick_edges(
        inside, vertical, left, right, borders, vertical_half, edge_scale, lists, inner
    )
    slot_adjoint = observe(
        exchange(outgoing), jacobian[0], inverse_r, channel_mask, group_instrument[0], observation_row
    )
    returned = exchange(slot_adjoint)
    scaled, left, right = gather(scale, lists, returned)
    borders, held = exchange_borders(*gather_edges(edge_scale, lists, returned), scaled)
    inner = finish_inside(held, vertical_half, control)
    return finish_edges(
        inside, scaled, left, right, borders, vertical_half, edge_control, inner
    )


def solution(mesh):
    placed = (
        P("lat", "lon", None),
        P(),
        P("lat", "lon", None),
        P(("lat", "lon"), None, None),
        P(),
        P(("lat", "lon"), None, None),
        P(("lat", "lon"), None),
        P(("lat", "lon"), None),
        P(("lat", "lon"), None, None),
    )
    return jax.shard_map(
        on_device, mesh=mesh, in_specs=placed, out_specs=P("lat", "lon", None), check_vma=False
    )
```

```python
import jax
import jax.numpy as jnp
from jax import lax
from jax.experimental import pallas as pl
from jax.experimental.pallas import tpu as pltpu
from jax.sharding import PartitionSpec as P

f32, bf16 = jnp.float32, jnp.bfloat16
weight_twice = 0.04
lanes_wide = 128
around = 48
parts = 4
mebi = 1024 * 1024
VMEM = pl.BlockSpec(memory_space=pltpu.VMEM)
SMEM = pl.BlockSpec(memory_space=pltpu.SMEM)
HBM = pl.BlockSpec(memory_space=pltpu.HBM)


def from_before(cells, axis):
    count = lax.axis_size(axis)
    return lax.ppermute(cells, axis, [(i, (i + 1) % count) for i in range(count)])


def from_after(cells, axis):
    count = lax.axis_size(axis)
    return lax.ppermute(cells, axis, [((i + 1) % count, i) for i in range(count)])


def exchange_borders(top, bottom, left, right, held):
    above = from_before(bottom, "lat")
    below = from_after(top, "lat")

    def taller(columns, at):
        column, rows, width = columns.shape
        under = jnp.swapaxes(below[:1, at], 0, 1)
        over = jnp.swapaxes(above[1:, at], 0, 1)
        gap = jnp.zeros((column, around - rows - 2, width), columns.dtype)
        return jnp.concatenate([columns, under, gap, over], axis=1)

    to_east, to_west, held = lax.optimization_barrier(
        (taller(right, slice(-2, None)), taller(left, slice(0, 2)), held)
    )
    west = from_before(to_east, "lon")
    east = from_after(to_west, "lon")
    return (above, below, west, east), held


def inside_poles():
    band = lax.axis_index("lat")
    ends = jnp.stack([band != 0, band != lax.axis_size("lat") - 1])
    return ends.astype(f32)


def stay(array):
    return pltpu.with_memory_space_constraint(array, pltpu.HBM)


def neighbours(before, here, after):
    ring = here.shape[0]
    return (here + before) + (after + (pltpu.roll(here, 1, 0) + pltpu.roll(here, ring - 1, 0)))


def lane_blocks(width):
    def run(body):
        @pl.loop(0, width // lanes_wide)
        def _(c):
            body(pl.ds(pl.multiple_of(c * lanes_wide, lanes_wide), lanes_wide))

    return run


def sum_twice_inside(center, at, emit):
    rows = center.shape[0]
    lines, sums = [center[0, :, at], center[1, :, at]], []
    for i in range(1, rows - 1):
        lines.append(center[i + 1, :, at])
        sums.append(neighbours(*lines))
        lines.pop(0)
        if len(sums) == 3:
            emit(i - 1, neighbours(*sums))
            sums.pop(0)


def sum_twice_edges(center, left, right, lines, sides, inside, at, emit):
    above, below = lines.at[0], lines.at[1]
    west, east = sides.at[0], sides.at[1]
    rows = center.shape[0]
    sublane = lax.broadcasted_iota(jnp.int32, (8, lanes_wide), 0)
    keep = jnp.where(sublane == 7, inside[0], jnp.where(sublane == 0, inside[1], 1.0))

    def cell(line, n, place):
        return jnp.broadcast_to(line[n, pl.ds(place, 1), at], (8, lanes_wide))

    def ends(e0, e1, w0, w1):
        return jnp.where(sublane < 1, e0, jnp.where(sublane < 2, e1, jnp.where(sublane < 7, w0, w1)))

    def row_line(own, i):
        if not -1 <= i <= rows:
            return jnp.concatenate([own, jnp.zeros((8, lanes_wide), f32)], axis=0)
        place = around - 1 if i < 0 else i
        tail = ends(cell(east, 0, place), cell(east, 1, place), cell(west, 0, place), cell(west, 1, place))
        if not 0 <= i < rows:
            tail = tail * inside[0 if i < 0 else 1]
        return jnp.concatenate([own, tail], axis=0)

    def column_line(own, j):
        tail = ends(cell(below, 0, j), cell(below, 1, j), cell(above, 0, j), cell(above, 1, j))
        return jnp.concatenate([own, tail], axis=0)

    def outer_column(side, n):
        after, before = cell(side, n, rows) * inside[1], cell(side, n, around - 1) * inside[0]
        return jnp.concatenate([side[n, :rows, at], ends(after, after, before, before)], axis=0)

    last = rows - 1
    edges = (
        [row_line(above[n, :, at], n - 2) for n in range(2)] + [row_line(center[n, :, at], n) for n in range(4)],
        [row_line(below[1 - n, :, at], rows + 1 - n) for n in range(2)]
        + [row_line(center[last - n, :, at], last - n) for n in range(4)],
        [outer_column(west, n) for n in range(2)] + [column_line(left[n, :, at], n) for n in range(4)],
        [outer_column(east, 1 - n) for n in range(2)]
        + [column_line(right[3 - n, :, at], last - n) for n in range(4)],
    )
    for e, edge in enumerate(edges):
        sums = [neighbours(*edge[n : n + 3]) for n in range(4)]
        if e < 2:
            sums[0] = sums[0] * inside[e]
        else:
            sums = [jnp.concatenate([s[:rows], s[rows:] * keep], axis=0) for s in sums]
        for n in range(2):
            emit(e, n, neighbours(*sums[n : n + 3])[:rows])


def edge_number(cell, rows, cols):
    row, col = cell // cols, cell % cols
    number = jnp.where(col < 2, 4 * cols + col * rows + row, -1)
    number = jnp.where(col >= cols - 2, 4 * cols + (2 + cols - 1 - col) * rows + row, number)
    number = jnp.where(row < 2, row * cols + col, number)
    return jnp.where(row >= rows - 2, (2 + rows - 1 - row) * cols + col, number)


def edge_lines(cells):
    rows, cols = cells.shape[0], cells.shape[1]
    return (
        [cells[0], cells[1], cells[rows - 1], cells[rows - 2]]
        + [cells[:, n, :] for n in (0, 1)]
        + [cells[:, cols - 1 - n, :] for n in (0, 1)]
    )


def borders_kernel(control, top, bottom, left, right, ends, flanks, sems):
    rows, cols, _ = control.shape
    copies = [
        pltpu.make_async_copy(control.at[pl.ds(0, 2)], ends.at[0], sems.at[0]),
        pltpu.make_async_copy(control.at[pl.ds(rows - 2, 2)], ends.at[1], sems.at[1]),
        pltpu.make_async_copy(control.at[:, pl.ds(0, 8)], flanks.at[0], sems.at[2]),
        pltpu.make_async_copy(control.at[:, pl.ds(cols - 8, 8)], flanks.at[1], sems.at[3]),
    ]
    for copy in copies:
        copy.start()
    for n, out in enumerate((top, bottom)):
        copies[n].wait()
        out[...] = ends[n].astype(bf16)
    for n, out in enumerate((left, right)):
        copies[2 + n].wait()
        for i in range(2):
            out[i] = flanks[n, :, 6 * n + i, :].astype(bf16)


def own_borders(control):
    rows, cols, width = control.shape
    side = jax.ShapeDtypeStruct((2, rows, width), bf16)
    border = jax.ShapeDtypeStruct((2, cols, width), bf16)
    return pl.pallas_call(
        borders_kernel,
        out_shape=(border, border, side, side),
        in_specs=[HBM],
        out_specs=(VMEM,) * 4,
        scratch_shapes=[
            pltpu.VMEM((2, 2, cols, width), f32),
            pltpu.VMEM((2, rows, 8, width), f32),
            pltpu.SemaphoreType.DMA((4,)),
        ],
        cost_estimate=pl.CostEstimate(flops=0, bytes_accessed=80 * rows * width, transcendentals=0),
        compiler_params=pltpu.CompilerParams(vmem_limit_bytes=8 * mebi),
    )(stay(control))


def lift_kernel(
    control,
    scale,
    vertical_half,
    vertical,
    left,
    right,
    held_scale,
    edge_scale,
    edge_control,
    held,
    weights,
    sems,
):
    rows, cols, width = held.shape
    high = rows // parts

    def get(b):
        place = pl.ds(pl.multiple_of(b * high, high), high)
        return pltpu.make_async_copy(control.at[place], held.at[place], sems.at[b])

    factor = pltpu.make_async_copy(vertical_half, weights, sems.at[parts])
    keep = pltpu.make_async_copy(scale, held_scale, sems.at[parts + 1])
    factor.start()
    for b in range(parts):
        get(b).start()
    keep.start()
    factor.wait()

    @pl.loop(0, parts)
    def _(b):
        get(b).wait()
        place = pl.ds(pl.multiple_of(b * high, high), high)
        cells = held[place].astype(bf16)
        vertical[place] = lax.dot_general(
            cells.reshape(high * cols, width),
            weights[...],
            (((1,), (1,)), ((), ())),
            preferred_element_type=f32,
        ).reshape(high, cols, width)

    for n in range(4):
        left[n] = vertical[:, n, :]
        right[n] = vertical[:, cols - 4 + n, :]
    for n, line in enumerate(edge_lines(held)):
        edge_control[n] = line
    keep.wait()
    for n, line in enumerate(edge_lines(held_scale)):
        edge_scale[n] = line


def lift(control, scale, vertical_half):
    rows, cols, width = control.shape
    side = jax.ShapeDtypeStruct((4, rows, width), f32)
    return pl.pallas_call(
        lift_kernel,
        out_shape=(
            jax.ShapeDtypeStruct(control.shape, f32),
            side,
            side,
            jax.ShapeDtypeStruct(scale.shape, scale.dtype),
            jax.ShapeDtypeStruct((8, rows, width), scale.dtype),
            jax.ShapeDtypeStruct((8, rows, width), f32),
        ),
        in_specs=[HBM] * 3,
        out_specs=(VMEM,) * 6,
        scratch_shapes=[
            pltpu.VMEM(control.shape, f32),
            pltpu.VMEM(vertical_half.shape, bf16),
            pltpu.SemaphoreType.DMA((parts + 2,)),
        ],
        cost_estimate=pl.CostEstimate(
            flops=2 * rows * cols * width * width, bytes_accessed=6 * rows * cols * width, transcendentals=0
        ),
        compiler_params=pltpu.CompilerParams(vmem_limit_bytes=16 * mebi),
    )(stay(control), stay(scale), stay(vertical_half))


def pick_inside_kernel(center, scale, lists, outgoing, state):
    rows, cols, width = center.shape
    for i in (0, 1, rows - 2, rows - 1):
        state[i * cols : (i + 1) * cols] = jnp.zeros((cols, width), bf16)

    @lane_blocks(width)
    def _(at):
        def emit(i, values):
            own = scale[i, :, at].astype(f32) * weight_twice
            state[i * cols : (i + 1) * cols, at] = (own * values).astype(bf16)

        sum_twice_inside(center, at, emit)

    cells = rows * cols
    count = lists.shape[2]
    lane = lax.broadcasted_iota(jnp.int32, (count, lanes_wide), 1)

    @pl.loop(0, parts)
    def _(b):
        cell = lists[b]
        inner = jnp.where(edge_number(cell, rows, cols) < 0, cell, -1)
        wanted = jnp.broadcast_to(inner, (lanes_wide, count)).T
        picker = jnp.concatenate(
            [jnp.where(wanted - t == lane, 1.0, 0.0).astype(bf16) for t in range(0, cells, lanes_wide)],
            axis=1,
        )
        place = pl.ds(pl.multiple_of(b * count, count), count)
        outgoing[place, :] = jnp.dot(picker, state[...], preferred_element_type=f32).astype(bf16)


def pick_inside(center, scale, lists):
    rows, cols, width = center.shape
    slots = lists.size
    return pl.pallas_call(
        pick_inside_kernel,
        out_shape=jax.ShapeDtypeStruct((slots, width), bf16),
        in_specs=[VMEM] * 3,
        out_specs=VMEM,
        scratch_shapes=[pltpu.VMEM((rows * cols, width), bf16)],
        cost_estimate=pl.CostEstimate(
            flops=2 * slots * rows * cols * width, bytes_accessed=4 * slots * width, transcendentals=0
        ),
        compiler_params=pltpu.CompilerParams(vmem_limit_bytes=16 * mebi),
    )(center, scale, lists)


def pick_edges_kernel(
    inside,
    center,
    left,
    right,
    above,
    below,
    west,
    east,
    vertical_half,
    edge_scale,
    lists,
    inner,
    outgoing,
    lines,
    sides,
    state,
):
    rows, cols, width = center.shape

    borders = [border[...].reshape(-1, width) for border in (above, below, west, east)]
    lifted = lax.dot_general(
        jnp.concatenate(borders, axis=0),
        vertical_half[...],
        (((1,), (1,)), ((), ())),
        preferred_element_type=f32,
    )
    start = 0
    for n, border in enumerate((above, below, west, east)):
        part = lifted[start : start + 2 * border.shape[1]].reshape(border.shape)
        start += 2 * border.shape[1]
        if n < 2:
            lines[n] = part * inside[n]
        else:
            sides[n - 2] = part

    @lane_blocks(width)
    def _(at):
        def emit(e, n, values):
            place = 2 * e + n
            own = edge_scale[place, :, at].astype(f32) * weight_twice
            state[place * rows : (place + 1) * rows, at] = (own * values).astype(bf16)

        sum_twice_edges(center, left, right, lines, sides, inside, at, emit)

    count = lists.shape[2]
    edges = state.shape[0]
    lane = lax.broadcasted_iota(jnp.int32, (count, lanes_wide), 1)

    @pl.loop(0, parts)
    def _(b):
        number = edge_number(lists[b], rows, cols)
        wanted = jnp.broadcast_to(number, (lanes_wide, count)).T
        picker = jnp.concatenate(
            [jnp.where(wanted - t == lane, 1.0, 0.0).astype(bf16) for t in range(0, edges, lanes_wide)],
            axis=1,
        )
        place = pl.ds(pl.multiple_of(b * count, count), count)
        edge = jnp.dot(picker, state[...], preferred_element_type=f32)
        outgoing[place, :] = (inner[place, :].astype(f32) + edge).astype(bf16)


def pick_edges(inside, center, left, right, borders, vertical_half, edge_scale, lists, inner):
    rows, cols, width = center.shape
    slots = lists.size
    edges = 8 * rows
    return pl.pallas_call(
        pick_edges_kernel,
        out_shape=jax.ShapeDtypeStruct((slots, width), bf16),
        in_specs=[SMEM] + [VMEM] * 11,
        out_specs=VMEM,
        scratch_shapes=[
            pltpu.VMEM((2, 2, cols, width), f32),
            pltpu.VMEM((2, 2, around, width), f32),
            pltpu.VMEM((edges, width), bf16),
        ],
        cost_estimate=pl.CostEstimate(
            flops=2 * slots * edges * width, bytes_accessed=4 * slots * width, transcendentals=0
        ),
        compiler_params=pltpu.CompilerParams(vmem_limit_bytes=16 * mebi),
    )(inside, center, left, right, *borders, vertical_half, edge_scale, lists, inner)


def observe_kernel(
    instrument, jacobian, inverse_r, used, slots, received, adjoint, weights, tables, collected, total
):
    rows, width = received.shape
    _, groups, channels = used.shape
    observes = slots.shape[2]
    half = rows // 2
    step = rows // parts
    together = tables.shape[1]
    rounds = groups // together

    for n in range(inverse_r.shape[0]):
        whole = inverse_r[n]
        high = whole.astype(bf16)
        low = (whole - high.astype(f32)).astype(bf16)
        both = jnp.concatenate([high, low], axis=1)
        weights[n] = jnp.concatenate([both, both], axis=0)

    def pair(q, p):
        start = (q * together + 2 * p) * channels
        return jacobian[start : start + 2 * channels, :]

    def predict(q):
        table = tables.at[q % 2]
        for p in range(together // 2):
            for b in range(half // step):
                for n in range(2):
                    start = n * half + b * step
                    predicted = lax.dot_general(
                        received[start : start + step, :],
                        pair(q, p),
                        (((1,), (1,)), ((), ())),
                        preferred_element_type=f32,
                    ).astype(bf16)
                    for i in range(2):
                        table[2 * p + i, b * step : (b + 1) * step, n * channels : (n + 1) * channels] = (
                            predicted[:, i * channels : (i + 1) * channels]
                        )

    lane = lax.broadcasted_iota(jnp.int32, (observes, channels), 1)
    position = lax.broadcasted_iota(jnp.int32, (half, observes), 0)

    def group(g, table):
        slot = slots[0, g : g + 1, :]
        wanted = jnp.broadcast_to(slot, (channels, observes)).T
        upper = wanted >= half
        local = jnp.where(upper, wanted - half, wanted)
        picker = jnp.concatenate(
            [jnp.where(local - t == lane, 1.0, 0.0).astype(bf16) for t in range(0, half, channels)],
            axis=1,
        )
        found = jnp.dot(picker, table[...], preferred_element_type=f32)
        mask = used[0, g : g + 1, :].astype(f32)
        model = jnp.where(upper, found[:, channels:], found[:, :channels]) * mask
        high = model.astype(bf16)
        low = (model - high.astype(f32)).astype(bf16)
        products = jnp.dot(
            jnp.concatenate([high, low], axis=1), weights[instrument[g]], preferred_element_type=f32
        )
        weighted = (products[:, :channels] + products[:, channels:]) * mask
        split = jnp.concatenate(
            [jnp.where(upper, 0.0, weighted), jnp.where(upper, weighted, 0.0)], axis=1
        ).astype(bf16)
        placer = jnp.where(position == jnp.where(slot >= half, slot - half, slot), 1.0, 0.0).astype(bf16)
        return jnp.dot(placer, split, preferred_element_type=f32).astype(bf16)

    def collect(q):
        for i in range(together):
            sums = group(q * together + i, tables.at[q % 2, i])
            columns = slice(i % 2 * channels, (i % 2 + 1) * channels)
            collected[q % 2, i // 2, :half, columns] = sums[:, :channels]
            collected[q % 2, i // 2, half:, columns] = sums[:, channels:]

    def spread(q):
        for b in range(parts):
            at = slice(b * step, (b + 1) * step)
            part = jnp.zeros((step, width), f32)
            for p in range(together // 2):
                part += jnp.dot(collected[q % 2, p, at], pair(q, p), preferred_element_type=f32)
            if q:
                part += total[at]
            if q < rounds - 1:
                total[at] = part
            else:
                adjoint[at] = part.astype(bf16)

    for q in range(rounds + 2):
        if q < rounds:
            predict(q)
        if q >= 2:
            spread(q - 2)
        if 1 <= q <= rounds:
            collect(q - 1)


def observe(received, weights, inverse_r, used, instrument, slots):
    rows, width = received.shape
    _, groups, channels = used.shape
    together = 4
    flops = 4 * rows * width * groups * channels + 4 * slots.size * rows * channels
    return pl.pallas_call(
        observe_kernel,
        out_shape=jax.ShapeDtypeStruct((rows, width), bf16),
        in_specs=[SMEM] + [VMEM] * 5,
        out_specs=VMEM,
        scratch_shapes=[
            pltpu.VMEM((inverse_r.shape[0], 2 * channels, 2 * channels), bf16),
            pltpu.VMEM((2, together, rows // 2, 2 * channels), bf16),
            pltpu.VMEM((2, together // 2, rows, 2 * channels), bf16),
            pltpu.VMEM((rows, width), f32),
        ],
        cost_estimate=pl.CostEstimate(flops=flops, bytes_accessed=6 * rows * width, transcendentals=0),
        compiler_params=pltpu.CompilerParams(vmem_limit_bytes=40 * mebi),
    )(
        instrument,
        weights,
        inverse_r,
        used,
        slots,
        received,
    )


def gather_edges_kernel(edge_scale, lists, returned, top, bottom, left, right):
    lines, rows, width = edge_scale.shape
    count = lists.shape[2]
    edges = lines * rows
    number = lax.broadcasted_iota(jnp.int32, (edges, count), 0)
    line, position = number // rows, number % rows
    depth = jnp.where(line % 4 < 2, line % 4, rows + 1 - line % 4)
    cell = jnp.where(line < 4, depth * rows + position, position * rows + depth)
    total = jnp.zeros((edges, width), f32)
    for b in range(parts):
        placer = jnp.where(cell == lists[b], 1.0, 0.0).astype(bf16)
        total += jnp.dot(placer, returned[b * count : (b + 1) * count, :], preferred_element_type=f32)
    scaled = (total.reshape(lines, rows, width) * edge_scale[...].astype(f32)).astype(bf16)
    for n in range(2):
        top[n] = scaled[n]
        bottom[1 - n] = scaled[2 + n]
        left[n] = scaled[4 + n]
        right[1 - n] = scaled[6 + n]


def gather_edges(edge_scale, lists, returned):
    lines, rows, width = edge_scale.shape
    slots = lists.size
    border = jax.ShapeDtypeStruct((2, rows, width), bf16)
    return pl.pallas_call(
        gather_edges_kernel,
        out_shape=(border,) * 4,
        in_specs=[VMEM] * 3,
        out_specs=(VMEM,) * 4,
        cost_estimate=pl.CostEstimate(
            flops=2 * slots * lines * rows * width, bytes_accessed=2 * slots * width, transcendentals=0
        ),
        compiler_params=pltpu.CompilerParams(vmem_limit_bytes=16 * mebi),
    )(edge_scale, lists, returned)


def gather_kernel(scale, lists, returned, scaled, left, right):
    rows, cols, width = scaled.shape
    count = lists.shape[2]
    high = rows // parts
    step = high * cols
    cell = lax.broadcasted_iota(jnp.int32, (step, count), 0)

    @pl.loop(0, parts)
    def _(m):
        total = jnp.zeros((step, width), f32)
        for b in range(parts):
            placer = jnp.where(cell == lists[b] - m * step, 1.0, 0.0).astype(bf16)
            total += jnp.dot(placer, returned[b * count : (b + 1) * count, :], preferred_element_type=f32)
        at = pl.ds(m * high, high)
        scaled[at] = total.reshape(high, cols, width) * scale[at].astype(f32)

    for n in range(4):
        left[n] = scaled[:, n, :]
        right[n] = scaled[:, cols - 4 + n, :]


def gather(scale, lists, returned):
    rows, cols, width = scale.shape
    slots = lists.size
    side = jax.ShapeDtypeStruct((4, rows, width), f32)
    return pl.pallas_call(
        gather_kernel,
        out_shape=(jax.ShapeDtypeStruct(scale.shape, f32), side, side),
        in_specs=[VMEM] * 3,
        out_specs=(VMEM,) * 3,
        cost_estimate=pl.CostEstimate(
            flops=slots * rows * cols * width // 2, bytes_accessed=slots * width, transcendentals=0
        ),
        compiler_params=pltpu.CompilerParams(vmem_limit_bytes=16 * mebi),
    )(scale, lists, returned)


def finish_inside_kernel(center, vertical_half, control, product, back):
    rows, cols, width = center.shape
    for i in (0, 1, rows - 2, rows - 1):
        back[i * cols : (i + 1) * cols] = jnp.zeros((cols, width), bf16)

    @lane_blocks(width)
    def _(at):
        def emit(i, values):
            back[i * cols : (i + 1) * cols, at] = (weight_twice * values).astype(bf16)

        sum_twice_inside(center, at, emit)

    high = rows // parts

    @pl.loop(0, parts)
    def _(b):
        place = pl.ds(pl.multiple_of(b * high * cols, high * cols), high * cols)
        result = jnp.dot(back[place, :], vertical_half[...], preferred_element_type=f32)
        at = pl.ds(b * high, high)
        product[at] = control[at] + result.reshape(high, cols, width)


def finish_inside(center, vertical_half, control):
    rows, cols, width = center.shape
    return pl.pallas_call(
        finish_inside_kernel,
        out_shape=jax.ShapeDtypeStruct(control.shape, f32),
        in_specs=[VMEM] * 3,
        out_specs=VMEM,
        scratch_shapes=[pltpu.VMEM((rows * cols, width), bf16)],
        cost_estimate=pl.CostEstimate(
            flops=2 * rows * cols * width * width, bytes_accessed=8 * rows * cols * width, transcendentals=0
        ),
        compiler_params=pltpu.CompilerParams(vmem_limit_bytes=16 * mebi),
    )(center, vertical_half, control)


def finish_edges_kernel(
    inside,
    center,
    left,
    right,
    above,
    below,
    west,
    east,
    vertical_half,
    edge_control,
    inner,
    product,
    lines,
    sides,
    back,
    ends,
    flanks,
    sems,
):
    rows, cols, width = center.shape
    body = pl.ds(2, rows - 4)

    def put(source, place, n):
        copy = pltpu.make_async_copy(source, product.at[place], sems.at[n])
        copy.start()
        return copy

    copies = [put(inner.at[body, pl.ds(8, cols - 16)], (body, pl.ds(8, cols - 16)), 0)]
    for n, border in enumerate((above, below)):
        lines[n] = border[...].astype(f32) * inside[n]
    for n, border in enumerate((west, east)):
        sides[n] = border[...].astype(f32)

    @lane_blocks(width)
    def _(at):
        def emit(e, n, values):
            place = 2 * e + n
            back[place * rows : (place + 1) * rows, at] = (weight_twice * values).astype(bf16)

        sum_twice_edges(center, left, right, lines, sides, inside, at, emit)

    result = jnp.dot(back[...], vertical_half[...], preferred_element_type=f32)
    edge = edge_control[...] + result.reshape(edge_control.shape)
    for n in range(2):
        ends[0, n] = edge[n]
        ends[1, 1 - n] = edge[2 + n]
    copies.append(put(ends.at[0], pl.ds(0, 2), 1))
    copies.append(put(ends.at[1], pl.ds(rows - 2, 2), 2))
    sublane = lax.broadcasted_iota(jnp.int32, (8, width), 0)
    for side in range(2):
        start = side * (cols - 8)
        for i in range(2, rows - 2):
            block = inner[i, start : start + 8, :]
            for n in range(2):
                outer = jnp.broadcast_to(edge[4 + 2 * side + n, i : i + 1, :], (8, width))
                block = jnp.where(sublane == (n if side == 0 else 7 - n), outer, block)
            flanks[side, i - 2] = block
        copies.append(put(flanks.at[side], (body, pl.ds(start, 8)), 3 + side))
    for copy in copies:
        copy.wait()


def finish_edges(inside, center, left, right, borders, vertical_half, edge_control, inner):
    rows, cols, width = center.shape
    return pl.pallas_call(
        finish_edges_kernel,
        out_shape=jax.ShapeDtypeStruct(inner.shape, f32),
        in_specs=[SMEM] + [VMEM] * 10,
        out_specs=HBM,
        scratch_shapes=[
            pltpu.VMEM((2, 2, cols, width), f32),
            pltpu.VMEM((2, 2, around, width), f32),
            pltpu.VMEM((8 * rows, width), bf16),
            pltpu.VMEM((2, 2, cols, width), f32),
            pltpu.VMEM((2, rows - 4, 8, width), f32),
            pltpu.SemaphoreType.DMA((5,)),
        ],
        cost_estimate=pl.CostEstimate(
            flops=16 * rows * width * width, bytes_accessed=4 * rows * cols * width, transcendentals=0
        ),
        compiler_params=pltpu.CompilerParams(vmem_limit_bytes=16 * mebi),
    )(inside, center, left, right, *borders, vertical_half, edge_control, inner)


def on_device(
    control,
    vertical_half,
    error_scale,
    jacobian,
    inverse_r,
    channel_mask,
    group_instrument,
    outbound_columns,
    observation_row,
):
    rows, cols, width = control.shape
    devices = lax.axis_size("lat") * lax.axis_size("lon")
    slots = outbound_columns.size
    lists = outbound_columns.reshape(parts, 1, slots // parts)
    inside = inside_poles()

    def exchange(columns):
        return lax.all_to_all(
            columns.reshape(devices, slots // devices, width),
            ("lat", "lon"),
            split_axis=0,
            concat_axis=0,
            tiled=True,
        ).reshape(slots, width)

    own = own_borders(control)
    vertical, left, right, scale, edge_scale, edge_control = lift(control, error_scale, vertical_half)
    borders, held = exchange_borders(*own, vertical)
    inner = pick_inside(held, scale, lists)
    outgoing = pick_edges(
        inside, vertical, left, right, borders, vertical_half, edge_scale, lists, inner
    )
    slot_adjoint = observe(
        exchange(outgoing), jacobian[0], inverse_r, channel_mask, group_instrument[0], observation_row
    )
    returned = exchange(slot_adjoint)
    scaled, left, right = gather(scale, lists, returned)
    borders, held = exchange_borders(*gather_edges(edge_scale, lists, returned), scaled)
    inner = finish_inside(held, vertical_half, control)
    return finish_edges(
        inside, scaled, left, right, borders, vertical_half, edge_control, inner
    )


def solution(mesh):
    placed = (
        P("lat", "lon", None),
        P(),
        P("lat", "lon", None),
        P(("lat", "lon"), None, None),
        P(),
        P(("lat", "lon"), None, None),
        P(("lat", "lon"), None),
        P(("lat", "lon"), None),
        P(("lat", "lon"), None, None),
    )
    return jax.shard_map(
        on_device, mesh=mesh, in_specs=placed, out_specs=P("lat", "lon", None), check_vma=False
    )
```

```python
import jax
import jax.numpy as jnp
from jax import lax
from jax.experimental import pallas as pl
from jax.experimental.pallas import tpu as pltpu
from jax.sharding import PartitionSpec as P

f32, bf16 = jnp.float32, jnp.bfloat16
weight_twice = 0.04
lanes_wide = 128
around = 48
parts = 4
mebi = 1024 * 1024
VMEM = pl.BlockSpec(memory_space=pltpu.VMEM)
SMEM = pl.BlockSpec(memory_space=pltpu.SMEM)
HBM = pl.BlockSpec(memory_space=pltpu.HBM)


def from_before(cells, axis):
    count = lax.axis_size(axis)
    return lax.ppermute(cells, axis, [(i, (i + 1) % count) for i in range(count)])


def from_after(cells, axis):
    count = lax.axis_size(axis)
    return lax.ppermute(cells, axis, [((i + 1) % count, i) for i in range(count)])


def exchange_borders(top, bottom, left, right, held):
    above = from_before(bottom, "lat")
    below = from_after(top, "lat")

    def taller(columns, at):
        column, rows, width = columns.shape
        under = jnp.swapaxes(below[:1, at], 0, 1)
        over = jnp.swapaxes(above[1:, at], 0, 1)
        gap = jnp.zeros((column, around - rows - 2, width), columns.dtype)
        return jnp.concatenate([columns, under, gap, over], axis=1)

    to_east, to_west, held = lax.optimization_barrier(
        (taller(right, slice(-2, None)), taller(left, slice(0, 2)), held)
    )
    west = from_before(to_east, "lon")
    east = from_after(to_west, "lon")
    return (above, below, west, east), held


def inside_poles():
    band = lax.axis_index("lat")
    ends = jnp.stack([band != 0, band != lax.axis_size("lat") - 1])
    return ends.astype(f32)


def stay(array):
    return pltpu.with_memory_space_constraint(array, pltpu.HBM)


def neighbours(before, here, after):
    ring = here.shape[0]
    return (here + before) + (after + (pltpu.roll(here, 1, 0) + pltpu.roll(here, ring - 1, 0)))


def lane_blocks(width):
    def run(body):
        @pl.loop(0, width // lanes_wide)
        def _(c):
            body(pl.ds(pl.multiple_of(c * lanes_wide, lanes_wide), lanes_wide))

    return run


def sum_twice_inside(center, at, emit):
    rows = center.shape[0]
    lines, sums = [center[0, :, at], center[1, :, at]], []
    for i in range(1, rows - 1):
        lines.append(center[i + 1, :, at])
        sums.append(neighbours(*lines))
        lines.pop(0)
        if len(sums) == 3:
            emit(i - 1, neighbours(*sums))
            sums.pop(0)


def sum_twice_edges(center, left, right, lines, sides, inside, at, emit):
    above, below = lines.at[0], lines.at[1]
    west, east = sides.at[0], sides.at[1]
    rows = center.shape[0]
    sublane = lax.broadcasted_iota(jnp.int32, (8, lanes_wide), 0)
    keep = jnp.where(sublane == 7, inside[0], jnp.where(sublane == 0, inside[1], 1.0))

    def cell(line, n, place):
        return jnp.broadcast_to(line[n, pl.ds(place, 1), at], (8, lanes_wide))

    def ends(e0, e1, w0, w1):
        return jnp.where(sublane < 1, e0, jnp.where(sublane < 2, e1, jnp.where(sublane < 7, w0, w1)))

    def row_line(own, i):
        if not -1 <= i <= rows:
            return jnp.concatenate([own, jnp.zeros((8, lanes_wide), f32)], axis=0)
        place = around - 1 if i < 0 else i
        tail = ends(cell(east, 0, place), cell(east, 1, place), cell(west, 0, place), cell(west, 1, place))
        if not 0 <= i < rows:
            tail = tail * inside[0 if i < 0 else 1]
        return jnp.concatenate([own, tail], axis=0)

    def column_line(own, j):
        tail = ends(cell(below, 0, j), cell(below, 1, j), cell(above, 0, j), cell(above, 1, j))
        return jnp.concatenate([own, tail], axis=0)

    def outer_column(side, n):
        after, before = cell(side, n, rows) * inside[1], cell(side, n, around - 1) * inside[0]
        return jnp.concatenate([side[n, :rows, at], ends(after, after, before, before)], axis=0)

    last = rows - 1
    edges = (
        [row_line(above[n, :, at], n - 2) for n in range(2)] + [row_line(center[n, :, at], n) for n in range(4)],
        [row_line(below[1 - n, :, at], rows + 1 - n) for n in range(2)]
        + [row_line(center[last - n, :, at], last - n) for n in range(4)],
        [outer_column(west, n) for n in range(2)] + [column_line(left[n, :, at], n) for n in range(4)],
        [outer_column(east, 1 - n) for n in range(2)]
        + [column_line(right[3 - n, :, at], last - n) for n in range(4)],
    )
    for e, edge in enumerate(edges):
        sums = [neighbours(*edge[n : n + 3]) for n in range(4)]
        if e < 2:
            sums[0] = sums[0] * inside[e]
        else:
            sums = [jnp.concatenate([s[:rows], s[rows:] * keep], axis=0) for s in sums]
        for n in range(2):
            emit(e, n, neighbours(*sums[n : n + 3])[:rows])


def edge_number(cell, rows, cols):
    row, col = cell // cols, cell % cols
    number = jnp.where(col < 2, 4 * cols + col * rows + row, -1)
    number = jnp.where(col >= cols - 2, 4 * cols + (2 + cols - 1 - col) * rows + row, number)
    number = jnp.where(row < 2, row * cols + col, number)
    return jnp.where(row >= rows - 2, (2 + rows - 1 - row) * cols + col, number)


def edge_lines(cells):
    rows, cols = cells.shape[0], cells.shape[1]
    return (
        [cells[0], cells[1], cells[rows - 1], cells[rows - 2]]
        + [cells[:, n, :] for n in (0, 1)]
        + [cells[:, cols - 1 - n, :] for n in (0, 1)]
    )


def borders_kernel(control, top, bottom, left, right, ends, flanks, sems):
    rows, cols, _ = control.shape
    copies = [
        pltpu.make_async_copy(control.at[pl.ds(0, 2)], ends.at[0], sems.at[0]),
        pltpu.make_async_copy(control.at[pl.ds(rows - 2, 2)], ends.at[1], sems.at[1]),
        pltpu.make_async_copy(control.at[:, pl.ds(0, 8)], flanks.at[0], sems.at[2]),
        pltpu.make_async_copy(control.at[:, pl.ds(cols - 8, 8)], flanks.at[1], sems.at[3]),
    ]
    for copy in copies:
        copy.start()
    for n, out in enumerate((top, bottom)):
        copies[n].wait()
        out[...] = ends[n].astype(bf16)
    for n, out in enumerate((left, right)):
        copies[2 + n].wait()
        for i in range(2):
            out[i] = flanks[n, :, 6 * n + i, :].astype(bf16)


def own_borders(control):
    rows, cols, width = control.shape
    side = jax.ShapeDtypeStruct((2, rows, width), bf16)
    border = jax.ShapeDtypeStruct((2, cols, width), bf16)
    return pl.pallas_call(
        borders_kernel,
        out_shape=(border, border, side, side),
        in_specs=[HBM],
        out_specs=(VMEM,) * 4,
        scratch_shapes=[
            pltpu.VMEM((2, 2, cols, width), f32),
            pltpu.VMEM((2, rows, 8, width), f32),
            pltpu.SemaphoreType.DMA((4,)),
        ],
        cost_estimate=pl.CostEstimate(flops=0, bytes_accessed=80 * rows * width, transcendentals=0),
        compiler_params=pltpu.CompilerParams(vmem_limit_bytes=8 * mebi),
    )(stay(control))


def lift_kernel(
    control,
    scale,
    vertical_half,
    vertical,
    left,
    right,
    held_scale,
    edge_scale,
    edge_control,
    held,
    weights,
    sems,
):
    rows, cols, width = held.shape
    high = rows // parts

    def get(b):
        place = pl.ds(pl.multiple_of(b * high, high), high)
        return pltpu.make_async_copy(control.at[place], held.at[place], sems.at[b])

    factor = pltpu.make_async_copy(vertical_half, weights, sems.at[parts])
    keep = pltpu.make_async_copy(scale, held_scale, sems.at[parts + 1])
    factor.start()
    for b in range(parts):
        get(b).start()
    keep.start()
    factor.wait()

    @pl.loop(0, parts)
    def _(b):
        get(b).wait()
        place = pl.ds(pl.multiple_of(b * high, high), high)
        cells = held[place].astype(bf16)
        vertical[place] = lax.dot_general(
            cells.reshape(high * cols, width),
            weights[...],
            (((1,), (1,)), ((), ())),
            preferred_element_type=f32,
        ).reshape(high, cols, width)

    for n in range(4):
        left[n] = vertical[:, n, :]
        right[n] = vertical[:, cols - 4 + n, :]
    for n, line in enumerate(edge_lines(held)):
        edge_control[n] = line
    keep.wait()
    for n, line in enumerate(edge_lines(held_scale)):
        edge_scale[n] = line


def lift(control, scale, vertical_half):
    rows, cols, width = control.shape
    side = jax.ShapeDtypeStruct((4, rows, width), f32)
    return pl.pallas_call(
        lift_kernel,
        out_shape=(
            jax.ShapeDtypeStruct(control.shape, f32),
            side,
            side,
            jax.ShapeDtypeStruct(scale.shape, scale.dtype),
            jax.ShapeDtypeStruct((8, rows, width), scale.dtype),
            jax.ShapeDtypeStruct((8, rows, width), f32),
        ),
        in_specs=[HBM] * 3,
        out_specs=(VMEM,) * 6,
        scratch_shapes=[
            pltpu.VMEM(control.shape, f32),
            pltpu.VMEM(vertical_half.shape, bf16),
            pltpu.SemaphoreType.DMA((parts + 2,)),
        ],
        cost_estimate=pl.CostEstimate(
            flops=2 * rows * cols * width * width, bytes_accessed=6 * rows * cols * width, transcendentals=0
        ),
        compiler_params=pltpu.CompilerParams(vmem_limit_bytes=16 * mebi),
    )(stay(control), stay(scale), stay(vertical_half))


def pick_inside_kernel(center, scale, lists, outgoing, state):
    rows, cols, width = center.shape
    for i in (0, 1, rows - 2, rows - 1):
        state[i * cols : (i + 1) * cols] = jnp.zeros((cols, width), bf16)

    @lane_blocks(width)
    def _(at):
        def emit(i, values):
            own = scale[i, :, at].astype(f32) * weight_twice
            state[i * cols : (i + 1) * cols, at] = (own * values).astype(bf16)

        sum_twice_inside(center, at, emit)

    cells = rows * cols
    count = lists.shape[2]
    lane = lax.broadcasted_iota(jnp.int32, (count, lanes_wide), 1)

    for b in range(parts):
        cell = lists[b]
        inner = jnp.where(edge_number(cell, rows, cols) < 0, cell, -1)
        wanted = jnp.broadcast_to(inner, (lanes_wide, count)).T
        picker = jnp.concatenate(
            [jnp.where(wanted - t == lane, 1.0, 0.0).astype(bf16) for t in range(0, cells, lanes_wide)],
            axis=1,
        )
        place = pl.ds(b * count, count)
        outgoing[place, :] = jnp.dot(picker, state[...], preferred_element_type=f32).astype(bf16)


def pick_inside(center, scale, lists):
    rows, cols, width = center.shape
    slots = lists.size
    return pl.pallas_call(
        pick_inside_kernel,
        out_shape=jax.ShapeDtypeStruct((slots, width), bf16),
        in_specs=[VMEM] * 3,
        out_specs=VMEM,
        scratch_shapes=[pltpu.VMEM((rows * cols, width), bf16)],
        cost_estimate=pl.CostEstimate(
            flops=2 * slots * rows * cols * width, bytes_accessed=4 * slots * width, transcendentals=0
        ),
        compiler_params=pltpu.CompilerParams(vmem_limit_bytes=16 * mebi),
    )(center, scale, lists)


def pick_edges_kernel(
    inside,
    center,
    left,
    right,
    above,
    below,
    west,
    east,
    vertical_half,
    edge_scale,
    lists,
    inner,
    outgoing,
    lines,
    sides,
    state,
):
    rows, cols, width = center.shape

    borders = [border[...].reshape(-1, width) for border in (above, below, west, east)]
    lifted = lax.dot_general(
        jnp.concatenate(borders, axis=0),
        vertical_half[...],
        (((1,), (1,)), ((), ())),
        preferred_element_type=f32,
    )
    start = 0
    for n, border in enumerate((above, below, west, east)):
        part = lifted[start : start + 2 * border.shape[1]].reshape(border.shape)
        start += 2 * border.shape[1]
        if n < 2:
            lines[n] = part * inside[n]
        else:
            sides[n - 2] = part

    @lane_blocks(width)
    def _(at):
        def emit(e, n, values):
            place = 2 * e + n
            own = edge_scale[place, :, at].astype(f32) * weight_twice
            state[place * rows : (place + 1) * rows, at] = (own * values).astype(bf16)

        sum_twice_edges(center, left, right, lines, sides, inside, at, emit)

    count = lists.shape[2]
    edges = state.shape[0]
    lane = lax.broadcasted_iota(jnp.int32, (count, lanes_wide), 1)

    for b in range(parts):
        number = edge_number(lists[b], rows, cols)
        wanted = jnp.broadcast_to(number, (lanes_wide, count)).T
        picker = jnp.concatenate(
            [jnp.where(wanted - t == lane, 1.0, 0.0).astype(bf16) for t in range(0, edges, lanes_wide)],
            axis=1,
        )
        place = pl.ds(b * count, count)
        edge = jnp.dot(picker, state[...], preferred_element_type=f32)
        outgoing[place, :] = (inner[place, :].astype(f32) + edge).astype(bf16)


def pick_edges(inside, center, left, right, borders, vertical_half, edge_scale, lists, inner):
    rows, cols, width = center.shape
    slots = lists.size
    edges = 8 * rows
    return pl.pallas_call(
        pick_edges_kernel,
        out_shape=jax.ShapeDtypeStruct((slots, width), bf16),
        in_specs=[SMEM] + [VMEM] * 11,
        out_specs=VMEM,
        scratch_shapes=[
            pltpu.VMEM((2, 2, cols, width), f32),
            pltpu.VMEM((2, 2, around, width), f32),
            pltpu.VMEM((edges, width), bf16),
        ],
        cost_estimate=pl.CostEstimate(
            flops=2 * slots * edges * width, bytes_accessed=4 * slots * width, transcendentals=0
        ),
        compiler_params=pltpu.CompilerParams(vmem_limit_bytes=16 * mebi),
    )(inside, center, left, right, *borders, vertical_half, edge_scale, lists, inner)


def observe_kernel(
    instrument, jacobian, inverse_r, used, slots, received, adjoint, weights, tables, collected, total
):
    rows, width = received.shape
    _, groups, channels = used.shape
    observes = slots.shape[2]
    half = rows // 2
    step = rows // parts
    together = tables.shape[1]
    rounds = groups // together

    for n in range(inverse_r.shape[0]):
        whole = inverse_r[n]
        high = whole.astype(bf16)
        low = (whole - high.astype(f32)).astype(bf16)
        both = jnp.concatenate([high, low], axis=1)
        weights[n] = jnp.concatenate([both, both], axis=0)

    def pair(q, p):
        start = (q * together + 2 * p) * channels
        return jacobian[start : start + 2 * channels, :]

    def predict(q):
        table = tables.at[q % 2]
        for p in range(together // 2):
            for b in range(half // step):
                for n in range(2):
                    start = n * half + b * step
                    predicted = lax.dot_general(
                        received[start : start + step, :],
                        pair(q, p),
                        (((1,), (1,)), ((), ())),
                        preferred_element_type=f32,
                    ).astype(bf16)
                    for i in range(2):
                        table[2 * p + i, b * step : (b + 1) * step, n * channels : (n + 1) * channels] = (
                            predicted[:, i * channels : (i + 1) * channels]
                        )

    lane = lax.broadcasted_iota(jnp.int32, (observes, channels), 1)
    position = lax.broadcasted_iota(jnp.int32, (half, observes), 0)

    def group(g, table):
        slot = slots[0, g : g + 1, :]
        wanted = jnp.broadcast_to(slot, (channels, observes)).T
        upper = wanted >= half
        local = jnp.where(upper, wanted - half, wanted)
        picker = jnp.concatenate(
            [jnp.where(local - t == lane, 1.0, 0.0).astype(bf16) for t in range(0, half, channels)],
            axis=1,
        )
        found = jnp.dot(picker, table[...], preferred_element_type=f32)
        mask = used[0, g : g + 1, :].astype(f32)
        model = jnp.where(upper, found[:, channels:], found[:, :channels]) * mask
        high = model.astype(bf16)
        low = (model - high.astype(f32)).astype(bf16)
        products = jnp.dot(
            jnp.concatenate([high, low], axis=1), weights[instrument[g]], preferred_element_type=f32
        )
        weighted = (products[:, :channels] + products[:, channels:]) * mask
        split = jnp.concatenate(
            [jnp.where(upper, 0.0, weighted), jnp.where(upper, weighted, 0.0)], axis=1
        ).astype(bf16)
        placer = jnp.where(position == jnp.where(slot >= half, slot - half, slot), 1.0, 0.0).astype(bf16)
        return jnp.dot(placer, split, preferred_element_type=f32).astype(bf16)

    def collect(q):
        for i in range(together):
            sums = group(q * together + i, tables.at[q % 2, i])
            columns = slice(i % 2 * channels, (i % 2 + 1) * channels)
            collected[q % 2, i // 2, :half, columns] = sums[:, :channels]
            collected[q % 2, i // 2, half:, columns] = sums[:, channels:]

    def spread(q):
        for b in range(parts):
            at = slice(b * step, (b + 1) * step)
            part = jnp.zeros((step, width), f32)
            for p in range(together // 2):
                part += jnp.dot(collected[q % 2, p, at], pair(q, p), preferred_element_type=f32)
            if q:
                part += total[at]
            if q < rounds - 1:
                total[at] = part
            else:
                adjoint[at] = part.astype(bf16)

    for q in range(rounds + 2):
        if q < rounds:
            predict(q)
        if q >= 2:
            spread(q - 2)
        if 1 <= q <= rounds:
            collect(q - 1)


def observe(received, weights, inverse_r, used, instrument, slots):
    rows, width = received.shape
    _, groups, channels = used.shape
    together = 4
    flops = 4 * rows * width * groups * channels + 4 * slots.size * rows * channels
    return pl.pallas_call(
        observe_kernel,
        out_shape=jax.ShapeDtypeStruct((rows, width), bf16),
        in_specs=[SMEM] + [VMEM] * 5,
        out_specs=VMEM,
        scratch_shapes=[
            pltpu.VMEM((inverse_r.shape[0], 2 * channels, 2 * channels), bf16),
            pltpu.VMEM((2, together, rows // 2, 2 * channels), bf16),
            pltpu.VMEM((2, together // 2, rows, 2 * channels), bf16),
            pltpu.VMEM((rows, width), f32),
        ],
        cost_estimate=pl.CostEstimate(flops=flops, bytes_accessed=6 * rows * width, transcendentals=0),
        compiler_params=pltpu.CompilerParams(vmem_limit_bytes=40 * mebi),
    )(
        instrument,
        weights,
        inverse_r,
        used,
        slots,
        received,
    )


def gather_edges_kernel(edge_scale, lists, returned, top, bottom, left, right):
    lines, rows, width = edge_scale.shape
    count = lists.shape[2]
    edges = lines * rows
    number = lax.broadcasted_iota(jnp.int32, (edges, count), 0)
    line, position = number // rows, number % rows
    depth = jnp.where(line % 4 < 2, line % 4, rows + 1 - line % 4)
    cell = jnp.where(line < 4, depth * rows + position, position * rows + depth)
    total = jnp.zeros((edges, width), f32)
    for b in range(parts):
        placer = jnp.where(cell == lists[b], 1.0, 0.0).astype(bf16)
        total += jnp.dot(placer, returned[b * count : (b + 1) * count, :], preferred_element_type=f32)
    scaled = (total.reshape(lines, rows, width) * edge_scale[...].astype(f32)).astype(bf16)
    for n in range(2):
        top[n] = scaled[n]
        bottom[1 - n] = scaled[2 + n]
        left[n] = scaled[4 + n]
        right[1 - n] = scaled[6 + n]


def gather_edges(edge_scale, lists, returned):
    lines, rows, width = edge_scale.shape
    slots = lists.size
    border = jax.ShapeDtypeStruct((2, rows, width), bf16)
    return pl.pallas_call(
        gather_edges_kernel,
        out_shape=(border,) * 4,
        in_specs=[VMEM] * 3,
        out_specs=(VMEM,) * 4,
        cost_estimate=pl.CostEstimate(
            flops=2 * slots * lines * rows * width, bytes_accessed=2 * slots * width, transcendentals=0
        ),
        compiler_params=pltpu.CompilerParams(vmem_limit_bytes=16 * mebi),
    )(edge_scale, lists, returned)


def gather_kernel(scale, lists, returned, scaled, left, right):
    rows, cols, width = scaled.shape
    count = lists.shape[2]
    cell = lax.broadcasted_iota(jnp.int32, (rows * cols, count), 0)
    total = jnp.zeros((rows * cols, width), f32)
    for b in range(parts):
        placer = jnp.where(cell == lists[b], 1.0, 0.0).astype(bf16)
        total += jnp.dot(placer, returned[b * count : (b + 1) * count, :], preferred_element_type=f32)
    scaled[...] = total.reshape(rows, cols, width) * scale[...].astype(f32)
    for n in range(4):
        left[n] = scaled[:, n, :]
        right[n] = scaled[:, cols - 4 + n, :]


def gather(scale, lists, returned):
    rows, cols, width = scale.shape
    slots = lists.size
    side = jax.ShapeDtypeStruct((4, rows, width), f32)
    return pl.pallas_call(
        gather_kernel,
        out_shape=(jax.ShapeDtypeStruct(scale.shape, f32), side, side),
        in_specs=[VMEM] * 3,
        out_specs=(VMEM,) * 3,
        cost_estimate=pl.CostEstimate(
            flops=slots * rows * cols * width // 2, bytes_accessed=slots * width, transcendentals=0
        ),
        compiler_params=pltpu.CompilerParams(vmem_limit_bytes=16 * mebi),
    )(scale, lists, returned)


def finish_inside_kernel(center, vertical_half, control, product, back):
    rows, cols, width = center.shape
    for i in (0, 1, rows - 2, rows - 1):
        back[i * cols : (i + 1) * cols] = jnp.zeros((cols, width), bf16)

    @lane_blocks(width)
    def _(at):
        def emit(i, values):
            back[i * cols : (i + 1) * cols, at] = (weight_twice * values).astype(bf16)

        sum_twice_inside(center, at, emit)

    high = rows // parts

    for b in range(parts):
        place = pl.ds(b * high * cols, high * cols)
        result = jnp.dot(back[place, :], vertical_half[...], preferred_element_type=f32)
        at = pl.ds(b * high, high)
        product[at] = control[at] + result.reshape(high, cols, width)


def finish_inside(center, vertical_half, control):
    rows, cols, width = center.shape
    return pl.pallas_call(
        finish_inside_kernel,
        out_shape=jax.ShapeDtypeStruct(control.shape, f32),
        in_specs=[VMEM] * 3,
        out_specs=VMEM,
        scratch_shapes=[pltpu.VMEM((rows * cols, width), bf16)],
        cost_estimate=pl.CostEstimate(
            flops=2 * rows * cols * width * width, bytes_accessed=8 * rows * cols * width, transcendentals=0
        ),
        compiler_params=pltpu.CompilerParams(vmem_limit_bytes=16 * mebi),
    )(center, vertical_half, control)


def finish_edges_kernel(
    inside,
    center,
    left,
    right,
    above,
    below,
    west,
    east,
    vertical_half,
    edge_control,
    inner,
    product,
    lines,
    sides,
    back,
    ends,
    flanks,
    sems,
):
    rows, cols, width = center.shape
    body = pl.ds(2, rows - 4)

    def put(source, place, n):
        copy = pltpu.make_async_copy(source, product.at[place], sems.at[n])
        copy.start()
        return copy

    copies = [put(inner.at[body, pl.ds(8, cols - 16)], (body, pl.ds(8, cols - 16)), 0)]
    for n, border in enumerate((above, below)):
        lines[n] = border[...].astype(f32) * inside[n]
    for n, border in enumerate((west, east)):
        sides[n] = border[...].astype(f32)

    @lane_blocks(width)
    def _(at):
        def emit(e, n, values):
            place = 2 * e + n
            back[place * rows : (place + 1) * rows, at] = (weight_twice * values).astype(bf16)

        sum_twice_edges(center, left, right, lines, sides, inside, at, emit)

    result = jnp.dot(back[...], vertical_half[...], preferred_element_type=f32)
    edge = edge_control[...] + result.reshape(edge_control.shape)
    for n in range(2):
        ends[0, n] = edge[n]
        ends[1, 1 - n] = edge[2 + n]
    copies.append(put(ends.at[0], pl.ds(0, 2), 1))
    copies.append(put(ends.at[1], pl.ds(rows - 2, 2), 2))
    sublane = lax.broadcasted_iota(jnp.int32, (8, width), 0)
    for side in range(2):
        start = side * (cols - 8)
        for i in range(2, rows - 2):
            block = inner[i, start : start + 8, :]
            for n in range(2):
                outer = jnp.broadcast_to(edge[4 + 2 * side + n, i : i + 1, :], (8, width))
                block = jnp.where(sublane == (n if side == 0 else 7 - n), outer, block)
            flanks[side, i - 2] = block
        copies.append(put(flanks.at[side], (body, pl.ds(start, 8)), 3 + side))
    for copy in copies:
        copy.wait()


def finish_edges(inside, center, left, right, borders, vertical_half, edge_control, inner):
    rows, cols, width = center.shape
    return pl.pallas_call(
        finish_edges_kernel,
        out_shape=jax.ShapeDtypeStruct(inner.shape, f32),
        in_specs=[SMEM] + [VMEM] * 10,
        out_specs=HBM,
        scratch_shapes=[
            pltpu.VMEM((2, 2, cols, width), f32),
            pltpu.VMEM((2, 2, around, width), f32),
            pltpu.VMEM((8 * rows, width), bf16),
            pltpu.VMEM((2, 2, cols, width), f32),
            pltpu.VMEM((2, rows - 4, 8, width), f32),
            pltpu.SemaphoreType.DMA((5,)),
        ],
        cost_estimate=pl.CostEstimate(
            flops=16 * rows * width * width, bytes_accessed=4 * rows * cols * width, transcendentals=0
        ),
        compiler_params=pltpu.CompilerParams(vmem_limit_bytes=16 * mebi),
    )(inside, center, left, right, *borders, vertical_half, edge_control, inner)


def on_device(
    control,
    vertical_half,
    error_scale,
    jacobian,
    inverse_r,
    channel_mask,
    group_instrument,
    outbound_columns,
    observation_row,
):
    rows, cols, width = control.shape
    devices = lax.axis_size("lat") * lax.axis_size("lon")
    slots = outbound_columns.size
    lists = outbound_columns.reshape(parts, 1, slots // parts)
    inside = inside_poles()

    def exchange(columns):
        return lax.all_to_all(
            columns.reshape(devices, slots // devices, width),
            ("lat", "lon"),
            split_axis=0,
            concat_axis=0,
            tiled=True,
        ).reshape(slots, width)

    own = own_borders(control)
    vertical, left, right, scale, edge_scale, edge_control = lift(control, error_scale, vertical_half)
    borders, held = exchange_borders(*own, vertical)
    inner = pick_inside(held, scale, lists)
    outgoing = pick_edges(
        inside, vertical, left, right, borders, vertical_half, edge_scale, lists, inner
    )
    slot_adjoint = observe(
        exchange(outgoing), jacobian[0], inverse_r, channel_mask, group_instrument[0], observation_row
    )
    returned = exchange(slot_adjoint)
    scaled, left, right = gather(scale, lists, returned)
    borders, held = exchange_borders(*gather_edges(edge_scale, lists, returned), scaled)
    inner = finish_inside(held, vertical_half, control)
    return finish_edges(
        inside, scaled, left, right, borders, vertical_half, edge_control, inner
    )


def solution(mesh):
    placed = (
        P("lat", "lon", None),
        P(),
        P("lat", "lon", None),
        P(("lat", "lon"), None, None),
        P(),
        P(("lat", "lon"), None, None),
        P(("lat", "lon"), None),
        P(("lat", "lon"), None),
        P(("lat", "lon"), None, None),
    )
    return jax.shard_map(
        on_device, mesh=mesh, in_specs=placed, out_specs=P("lat", "lon", None), check_vma=False
    )
```

```python
import jax
import jax.numpy as jnp
from jax import lax
from jax.experimental import pallas as pl
from jax.experimental.pallas import tpu as pltpu
from jax.sharding import PartitionSpec as P

f32, bf16 = jnp.float32, jnp.bfloat16
weight_twice = 0.04
lanes_wide = 128
around = 48
parts = 4
mebi = 1024 * 1024
VMEM = pl.BlockSpec(memory_space=pltpu.VMEM)
SMEM = pl.BlockSpec(memory_space=pltpu.SMEM)
HBM = pl.BlockSpec(memory_space=pltpu.HBM)


def from_before(cells, axis):
    count = lax.axis_size(axis)
    return lax.ppermute(cells, axis, [(i, (i + 1) % count) for i in range(count)])


def from_after(cells, axis):
    count = lax.axis_size(axis)
    return lax.ppermute(cells, axis, [((i + 1) % count, i) for i in range(count)])


def exchange_borders(top, bottom, left, right, held):
    above = from_before(bottom, "lat")
    below = from_after(top, "lat")

    def taller(columns, at):
        column, rows, width = columns.shape
        under = jnp.swapaxes(below[:1, at], 0, 1)
        over = jnp.swapaxes(above[1:, at], 0, 1)
        gap = jnp.zeros((column, around - rows - 2, width), columns.dtype)
        return jnp.concatenate([columns, under, gap, over], axis=1)

    to_east, to_west, held = lax.optimization_barrier(
        (taller(right, slice(-2, None)), taller(left, slice(0, 2)), held)
    )
    west = from_before(to_east, "lon")
    east = from_after(to_west, "lon")
    return (above, below, west, east), held


def inside_poles():
    band = lax.axis_index("lat")
    ends = jnp.stack([band != 0, band != lax.axis_size("lat") - 1])
    return ends.astype(f32)


def stay(array):
    return pltpu.with_memory_space_constraint(array, pltpu.HBM)


def neighbours(before, here, after):
    ring = here.shape[0]
    return (here + before) + (after + (pltpu.roll(here, 1, 0) + pltpu.roll(here, ring - 1, 0)))


def lane_blocks(width):
    def run(body):
        @pl.loop(0, width // lanes_wide)
        def _(c):
            body(pl.ds(pl.multiple_of(c * lanes_wide, lanes_wide), lanes_wide))

    return run


def sum_twice_inside(center, at, emit):
    rows = center.shape[0]
    lines, sums = [center[0, :, at], center[1, :, at]], []
    for i in range(1, rows - 1):
        lines.append(center[i + 1, :, at])
        sums.append(neighbours(*lines))
        lines.pop(0)
        if len(sums) == 3:
            emit(i - 1, neighbours(*sums))
            sums.pop(0)


def sum_twice_edges(center, left, right, lines, sides, inside, at, emit):
    above, below = lines.at[0], lines.at[1]
    west, east = sides.at[0], sides.at[1]
    rows = center.shape[0]
    sublane = lax.broadcasted_iota(jnp.int32, (8, lanes_wide), 0)
    keep = jnp.where(sublane == 7, inside[0], jnp.where(sublane == 0, inside[1], 1.0))

    def cell(line, n, place):
        return jnp.broadcast_to(line[n, pl.ds(place, 1), at], (8, lanes_wide))

    def ends(e0, e1, w0, w1):
        return jnp.where(sublane < 1, e0, jnp.where(sublane < 2, e1, jnp.where(sublane < 7, w0, w1)))

    def row_line(own, i):
        if not -1 <= i <= rows:
            return jnp.concatenate([own, jnp.zeros((8, lanes_wide), f32)], axis=0)
        place = around - 1 if i < 0 else i
        tail = ends(cell(east, 0, place), cell(east, 1, place), cell(west, 0, place), cell(west, 1, place))
        if not 0 <= i < rows:
            tail = tail * inside[0 if i < 0 else 1]
        return jnp.concatenate([own, tail], axis=0)

    def column_line(own, j):
        tail = ends(cell(below, 0, j), cell(below, 1, j), cell(above, 0, j), cell(above, 1, j))
        return jnp.concatenate([own, tail], axis=0)

    def outer_column(side, n):
        after, before = cell(side, n, rows) * inside[1], cell(side, n, around - 1) * inside[0]
        return jnp.concatenate([side[n, :rows, at], ends(after, after, before, before)], axis=0)

    last = rows - 1
    edges = (
        [row_line(above[n, :, at], n - 2) for n in range(2)] + [row_line(center[n, :, at], n) for n in range(4)],
        [row_line(below[1 - n, :, at], rows + 1 - n) for n in range(2)]
        + [row_line(center[last - n, :, at], last - n) for n in range(4)],
        [outer_column(west, n) for n in range(2)] + [column_line(left[n, :, at], n) for n in range(4)],
        [outer_column(east, 1 - n) for n in range(2)]
        + [column_line(right[3 - n, :, at], last - n) for n in range(4)],
    )
    for e, edge in enumerate(edges):
        sums = [neighbours(*edge[n : n + 3]) for n in range(4)]
        if e < 2:
            sums[0] = sums[0] * inside[e]
        else:
            sums = [jnp.concatenate([s[:rows], s[rows:] * keep], axis=0) for s in sums]
        for n in range(2):
            emit(e, n, neighbours(*sums[n : n + 3])[:rows])


def edge_number(cell, rows, cols):
    row, col = cell // cols, cell % cols
    number = jnp.where(col < 2, 4 * cols + col * rows + row, -1)
    number = jnp.where(col >= cols - 2, 4 * cols + (2 + cols - 1 - col) * rows + row, number)
    number = jnp.where(row < 2, row * cols + col, number)
    return jnp.where(row >= rows - 2, (2 + rows - 1 - row) * cols + col, number)


def edge_lines(cells):
    rows, cols = cells.shape[0], cells.shape[1]
    return (
        [cells[0], cells[1], cells[rows - 1], cells[rows - 2]]
        + [cells[:, n, :] for n in (0, 1)]
        + [cells[:, cols - 1 - n, :] for n in (0, 1)]
    )


def borders_kernel(control, top, bottom, left, right, ends, flanks, sems):
    rows, cols, _ = control.shape
    copies = [
        pltpu.make_async_copy(control.at[pl.ds(0, 2)], ends.at[0], sems.at[0]),
        pltpu.make_async_copy(control.at[pl.ds(rows - 2, 2)], ends.at[1], sems.at[1]),
        pltpu.make_async_copy(control.at[:, pl.ds(0, 8)], flanks.at[0], sems.at[2]),
        pltpu.make_async_copy(control.at[:, pl.ds(cols - 8, 8)], flanks.at[1], sems.at[3]),
    ]
    for copy in copies:
        copy.start()
    for n, out in enumerate((top, bottom)):
        copies[n].wait()
        out[...] = ends[n].astype(bf16)
    for n, out in enumerate((left, right)):
        copies[2 + n].wait()
        for i in range(2):
            out[i] = flanks[n, :, 6 * n + i, :].astype(bf16)


def own_borders(control):
    rows, cols, width = control.shape
    side = jax.ShapeDtypeStruct((2, rows, width), bf16)
    border = jax.ShapeDtypeStruct((2, cols, width), bf16)
    return pl.pallas_call(
        borders_kernel,
        out_shape=(border, border, side, side),
        in_specs=[HBM],
        out_specs=(VMEM,) * 4,
        scratch_shapes=[
            pltpu.VMEM((2, 2, cols, width), f32),
            pltpu.VMEM((2, rows, 8, width), f32),
            pltpu.SemaphoreType.DMA((4,)),
        ],
        cost_estimate=pl.CostEstimate(flops=0, bytes_accessed=80 * rows * width, transcendentals=0),
        compiler_params=pltpu.CompilerParams(vmem_limit_bytes=8 * mebi),
    )(stay(control))


def lift_kernel(
    control,
    scale,
    vertical_half,
    vertical,
    left,
    right,
    held_scale,
    edge_scale,
    edge_control,
    held,
    weights,
    sems,
):
    rows, cols, width = held.shape
    high = rows // parts

    def get(b):
        place = pl.ds(pl.multiple_of(b * high, high), high)
        return pltpu.make_async_copy(control.at[place], held.at[place], sems.at[b])

    factor = pltpu.make_async_copy(vertical_half, weights, sems.at[parts])
    keep = pltpu.make_async_copy(scale, held_scale, sems.at[parts + 1])
    factor.start()
    for b in range(parts):
        get(b).start()
    keep.start()
    factor.wait()

    @pl.loop(0, parts)
    def _(b):
        get(b).wait()
        place = pl.ds(pl.multiple_of(b * high, high), high)
        cells = held[place].astype(bf16)
        vertical[place] = lax.dot_general(
            cells.reshape(high * cols, width),
            weights[...],
            (((1,), (1,)), ((), ())),
            preferred_element_type=f32,
        ).reshape(high, cols, width)

    for n in range(4):
        left[n] = vertical[:, n, :]
        right[n] = vertical[:, cols - 4 + n, :]
    for n, line in enumerate(edge_lines(held)):
        edge_control[n] = line
    keep.wait()
    for n, line in enumerate(edge_lines(held_scale)):
        edge_scale[n] = line


def lift(control, scale, vertical_half):
    rows, cols, width = control.shape
    side = jax.ShapeDtypeStruct((4, rows, width), f32)
    return pl.pallas_call(
        lift_kernel,
        out_shape=(
            jax.ShapeDtypeStruct(control.shape, f32),
            side,
            side,
            jax.ShapeDtypeStruct(scale.shape, scale.dtype),
            jax.ShapeDtypeStruct((8, rows, width), scale.dtype),
            jax.ShapeDtypeStruct((8, rows, width), f32),
        ),
        in_specs=[HBM] * 3,
        out_specs=(VMEM,) * 6,
        scratch_shapes=[
            pltpu.VMEM(control.shape, f32),
            pltpu.VMEM(vertical_half.shape, bf16),
            pltpu.SemaphoreType.DMA((parts + 2,)),
        ],
        cost_estimate=pl.CostEstimate(
            flops=2 * rows * cols * width * width, bytes_accessed=6 * rows * cols * width, transcendentals=0
        ),
        compiler_params=pltpu.CompilerParams(vmem_limit_bytes=16 * mebi),
    )(stay(control), stay(scale), stay(vertical_half))


def pick_inside_kernel(center, scale, lists, outgoing, edge_picker, state):
    rows, cols, width = center.shape
    for i in (0, 1, rows - 2, rows - 1):
        state[i * cols : (i + 1) * cols] = jnp.zeros((cols, width), bf16)

    @lane_blocks(width)
    def _(at):
        def emit(i, values):
            own = scale[i, :, at].astype(f32) * weight_twice
            state[i * cols : (i + 1) * cols, at] = (own * values).astype(bf16)

        sum_twice_inside(center, at, emit)

    cells = rows * cols
    count = lists.shape[2]
    lane = lax.broadcasted_iota(jnp.int32, (count, lanes_wide), 1)

    for b in range(parts):
        cell = lists[b]
        number = edge_number(cell, rows, cols)
        inner = jnp.where(number < 0, cell, -1)
        edge = jnp.broadcast_to(number, (lanes_wide, count)).T
        for t in range(0, 8 * rows, lanes_wide):
            edge_picker[b * count : (b + 1) * count, t : t + lanes_wide] = jnp.where(
                edge - t == lane, 1.0, 0.0
            ).astype(bf16)
        wanted = jnp.broadcast_to(inner, (lanes_wide, count)).T
        picker = jnp.concatenate(
            [jnp.where(wanted - t == lane, 1.0, 0.0).astype(bf16) for t in range(0, cells, lanes_wide)],
            axis=1,
        )
        place = pl.ds(b * count, count)
        outgoing[place, :] = jnp.dot(picker, state[...], preferred_element_type=f32).astype(bf16)


def pick_inside(center, scale, lists):
    rows, cols, width = center.shape
    slots = lists.size
    return pl.pallas_call(
        pick_inside_kernel,
        out_shape=(
            jax.ShapeDtypeStruct((slots, width), bf16),
            jax.ShapeDtypeStruct((slots, 8 * rows), bf16),
        ),
        in_specs=[VMEM] * 3,
        out_specs=(VMEM, VMEM),
        scratch_shapes=[pltpu.VMEM((rows * cols, width), bf16)],
        cost_estimate=pl.CostEstimate(
            flops=2 * slots * rows * cols * width, bytes_accessed=4 * slots * width, transcendentals=0
        ),
        compiler_params=pltpu.CompilerParams(vmem_limit_bytes=16 * mebi),
    )(center, scale, lists)


def pick_edges_kernel(
    inside,
    center,
    left,
    right,
    above,
    below,
    west,
    east,
    vertical_half,
    edge_scale,
    picker,
    inner,
    outgoing,
    lines,
    sides,
    state,
):
    rows, cols, width = center.shape

    borders = [border[...].reshape(-1, width) for border in (above, below, west, east)]
    lifted = lax.dot_general(
        jnp.concatenate(borders, axis=0),
        vertical_half[...],
        (((1,), (1,)), ((), ())),
        preferred_element_type=f32,
    )
    start = 0
    for n, border in enumerate((above, below, west, east)):
        part = lifted[start : start + 2 * border.shape[1]].reshape(border.shape)
        start += 2 * border.shape[1]
        if n < 2:
            lines[n] = part * inside[n]
        else:
            sides[n - 2] = part

    @lane_blocks(width)
    def _(at):
        def emit(e, n, values):
            place = 2 * e + n
            own = edge_scale[place, :, at].astype(f32) * weight_twice
            state[place * rows : (place + 1) * rows, at] = (own * values).astype(bf16)

        sum_twice_edges(center, left, right, lines, sides, inside, at, emit)

    count = picker.shape[0] // parts
    for b in range(parts):
        place = pl.ds(b * count, count)
        edge = jnp.dot(picker[place, :], state[...], preferred_element_type=f32)
        outgoing[place, :] = inner[place, :] + edge.astype(bf16)


def pick_edges(inside, center, left, right, borders, vertical_half, edge_scale, picker, inner):
    rows, cols, width = center.shape
    slots = picker.shape[0]
    edges = 8 * rows
    return pl.pallas_call(
        pick_edges_kernel,
        out_shape=jax.ShapeDtypeStruct((slots, width), bf16),
        in_specs=[SMEM] + [VMEM] * 11,
        out_specs=VMEM,
        scratch_shapes=[
            pltpu.VMEM((2, 2, cols, width), f32),
            pltpu.VMEM((2, 2, around, width), f32),
            pltpu.VMEM((edges, width), bf16),
        ],
        cost_estimate=pl.CostEstimate(
            flops=2 * slots * edges * width, bytes_accessed=4 * slots * width, transcendentals=0
        ),
        compiler_params=pltpu.CompilerParams(vmem_limit_bytes=16 * mebi),
    )(inside, center, left, right, *borders, vertical_half, edge_scale, picker, inner)


def observe_kernel(
    instrument, jacobian, inverse_r, used, slots, received, adjoint, weights, tables, collected, total
):
    rows, width = received.shape
    _, groups, channels = used.shape
    observes = slots.shape[2]
    half = rows // 2
    step = rows // parts
    together = tables.shape[1]
    rounds = groups // together

    for n in range(inverse_r.shape[0]):
        whole = inverse_r[n]
        high = whole.astype(bf16)
        low = (whole - high.astype(f32)).astype(bf16)
        both = jnp.concatenate([high, low], axis=1)
        weights[n] = jnp.concatenate([both, both], axis=0)

    def pair(q, p):
        start = (q * together + 2 * p) * channels
        return jacobian[start : start + 2 * channels, :]

    def predict(q):
        table = tables.at[q % 2]
        for p in range(together // 2):
            for b in range(half // step):
                for n in range(2):
                    start = n * half + b * step
                    predicted = lax.dot_general(
                        received[start : start + step, :],
                        pair(q, p),
                        (((1,), (1,)), ((), ())),
                        preferred_element_type=f32,
                    ).astype(bf16)
                    for i in range(2):
                        table[2 * p + i, b * step : (b + 1) * step, n * channels : (n + 1) * channels] = (
                            predicted[:, i * channels : (i + 1) * channels]
                        )

    lane = lax.broadcasted_iota(jnp.int32, (observes, channels), 1)
    position = lax.broadcasted_iota(jnp.int32, (half, observes), 0)

    def group(g, table):
        slot = slots[0, g : g + 1, :]
        wanted = jnp.broadcast_to(slot, (channels, observes)).T
        upper = wanted >= half
        local = jnp.where(upper, wanted - half, wanted)
        picker = jnp.concatenate(
            [jnp.where(local - t == lane, 1.0, 0.0).astype(bf16) for t in range(0, half, channels)],
            axis=1,
        )
        found = jnp.dot(picker, table[...], preferred_element_type=f32)
        mask = used[0, g : g + 1, :].astype(f32)
        model = jnp.where(upper, found[:, channels:], found[:, :channels]) * mask
        high = model.astype(bf16)
        low = (model - high.astype(f32)).astype(bf16)
        products = jnp.dot(
            jnp.concatenate([high, low], axis=1), weights[instrument[g]], preferred_element_type=f32
        )
        weighted = (products[:, :channels] + products[:, channels:]) * mask
        split = jnp.concatenate(
            [jnp.where(upper, 0.0, weighted), jnp.where(upper, weighted, 0.0)], axis=1
        ).astype(bf16)
        placer = jnp.where(position == jnp.where(slot >= half, slot - half, slot), 1.0, 0.0).astype(bf16)
        return jnp.dot(placer, split, preferred_element_type=f32).astype(bf16)

    def collect(q):
        for i in range(together):
            sums = group(q * together + i, tables.at[q % 2, i])
            columns = slice(i % 2 * channels, (i % 2 + 1) * channels)
            collected[q % 2, i // 2, :half, columns] = sums[:, :channels]
            collected[q % 2, i // 2, half:, columns] = sums[:, channels:]

    def spread(q):
        for b in range(parts):
            at = slice(b * step, (b + 1) * step)
            part = jnp.zeros((step, width), f32)
            for p in range(together // 2):
                part += jnp.dot(collected[q % 2, p, at], pair(q, p), preferred_element_type=f32)
            if q:
                part += total[at]
            if q < rounds - 1:
                total[at] = part
            else:
                adjoint[at] = part.astype(bf16)

    for q in range(rounds + 2):
        if q < rounds:
            predict(q)
        if q >= 2:
            spread(q - 2)
        if 1 <= q <= rounds:
            collect(q - 1)


def observe(received, weights, inverse_r, used, instrument, slots):
    rows, width = received.shape
    _, groups, channels = used.shape
    together = 4
    flops = 4 * rows * width * groups * channels + 4 * slots.size * rows * channels
    return pl.pallas_call(
        observe_kernel,
        out_shape=jax.ShapeDtypeStruct((rows, width), bf16),
        in_specs=[SMEM] + [VMEM] * 5,
        out_specs=VMEM,
        scratch_shapes=[
            pltpu.VMEM((inverse_r.shape[0], 2 * channels, 2 * channels), bf16),
            pltpu.VMEM((2, together, rows // 2, 2 * channels), bf16),
            pltpu.VMEM((2, together // 2, rows, 2 * channels), bf16),
            pltpu.VMEM((rows, width), f32),
        ],
        cost_estimate=pl.CostEstimate(flops=flops, bytes_accessed=6 * rows * width, transcendentals=0),
        compiler_params=pltpu.CompilerParams(vmem_limit_bytes=40 * mebi),
    )(
        instrument,
        weights,
        inverse_r,
        used,
        slots,
        received,
    )


def gather_edges_kernel(edge_scale, lists, returned, top, bottom, left, right):
    lines, rows, width = edge_scale.shape
    count = lists.shape[2]
    edges = lines * rows
    number = lax.broadcasted_iota(jnp.int32, (edges, count), 0)
    line, position = number // rows, number % rows
    depth = jnp.where(line % 4 < 2, line % 4, rows + 1 - line % 4)
    cell = jnp.where(line < 4, depth * rows + position, position * rows + depth)
    total = jnp.zeros((edges, width), f32)
    for b in range(parts):
        placer = jnp.where(cell == lists[b], 1.0, 0.0).astype(bf16)
        total += jnp.dot(placer, returned[b * count : (b + 1) * count, :], preferred_element_type=f32)
    scaled = (total.reshape(lines, rows, width) * edge_scale[...].astype(f32)).astype(bf16)
    for n in range(2):
        top[n] = scaled[n]
        bottom[1 - n] = scaled[2 + n]
        left[n] = scaled[4 + n]
        right[1 - n] = scaled[6 + n]


def gather_edges(edge_scale, lists, returned):
    lines, rows, width = edge_scale.shape
    slots = lists.size
    border = jax.ShapeDtypeStruct((2, rows, width), bf16)
    return pl.pallas_call(
        gather_edges_kernel,
        out_shape=(border,) * 4,
        in_specs=[VMEM] * 3,
        out_specs=(VMEM,) * 4,
        cost_estimate=pl.CostEstimate(
            flops=2 * slots * lines * rows * width, bytes_accessed=2 * slots * width, transcendentals=0
        ),
        compiler_params=pltpu.CompilerParams(vmem_limit_bytes=16 * mebi),
    )(edge_scale, lists, returned)


def gather_kernel(scale, lists, returned, scaled, left, right):
    rows, cols, width = scaled.shape
    count = lists.shape[2]
    cell = lax.broadcasted_iota(jnp.int32, (rows * cols, count), 0)
    total = jnp.zeros((rows * cols, width), f32)
    for b in range(parts):
        placer = jnp.where(cell == lists[b], 1.0, 0.0).astype(bf16)
        total += jnp.dot(placer, returned[b * count : (b + 1) * count, :], preferred_element_type=f32)
    scaled[...] = total.reshape(rows, cols, width) * scale[...].astype(f32)
    for n in range(4):
        left[n] = scaled[:, n, :]
        right[n] = scaled[:, cols - 4 + n, :]


def gather(scale, lists, returned):
    rows, cols, width = scale.shape
    slots = lists.size
    side = jax.ShapeDtypeStruct((4, rows, width), f32)
    return pl.pallas_call(
        gather_kernel,
        out_shape=(jax.ShapeDtypeStruct(scale.shape, f32), side, side),
        in_specs=[VMEM] * 3,
        out_specs=(VMEM,) * 3,
        cost_estimate=pl.CostEstimate(
            flops=slots * rows * cols * width // 2, bytes_accessed=slots * width, transcendentals=0
        ),
        compiler_params=pltpu.CompilerParams(vmem_limit_bytes=16 * mebi),
    )(scale, lists, returned)


def finish_inside_kernel(center, vertical_half, control, product, back):
    rows, cols, width = center.shape
    for i in (0, 1, rows - 2, rows - 1):
        back[i * cols : (i + 1) * cols] = jnp.zeros((cols, width), bf16)

    @lane_blocks(width)
    def _(at):
        def emit(i, values):
            back[i * cols : (i + 1) * cols, at] = (weight_twice * values).astype(bf16)

        sum_twice_inside(center, at, emit)

    high = rows // parts

    for b in range(parts):
        place = pl.ds(b * high * cols, high * cols)
        result = jnp.dot(back[place, :], vertical_half[...], preferred_element_type=f32)
        at = pl.ds(b * high, high)
        product[at] = control[at] + result.reshape(high, cols, width)


def finish_inside(center, vertical_half, control):
    rows, cols, width = center.shape
    return pl.pallas_call(
        finish_inside_kernel,
        out_shape=jax.ShapeDtypeStruct(control.shape, f32),
        in_specs=[VMEM] * 3,
        out_specs=VMEM,
        scratch_shapes=[pltpu.VMEM((rows * cols, width), bf16)],
        cost_estimate=pl.CostEstimate(
            flops=2 * rows * cols * width * width, bytes_accessed=8 * rows * cols * width, transcendentals=0
        ),
        compiler_params=pltpu.CompilerParams(vmem_limit_bytes=16 * mebi),
    )(center, vertical_half, control)


def finish_edges_kernel(
    inside,
    center,
    left,
    right,
    above,
    below,
    west,
    east,
    vertical_half,
    edge_control,
    inner,
    product,
    lines,
    sides,
    back,
    ends,
    flanks,
    sems,
):
    rows, cols, width = center.shape
    body = pl.ds(2, rows - 4)

    def put(source, place, n):
        copy = pltpu.make_async_copy(source, product.at[place], sems.at[n])
        copy.start()
        return copy

    copies = [put(inner.at[body, pl.ds(8, cols - 16)], (body, pl.ds(8, cols - 16)), 0)]
    for n, border in enumerate((above, below)):
        lines[n] = border[...].astype(f32) * inside[n]
    for n, border in enumerate((west, east)):
        sides[n] = border[...].astype(f32)

    @lane_blocks(width)
    def _(at):
        def emit(e, n, values):
            place = 2 * e + n
            back[place * rows : (place + 1) * rows, at] = (weight_twice * values).astype(bf16)

        sum_twice_edges(center, left, right, lines, sides, inside, at, emit)

    result = jnp.dot(back[...], vertical_half[...], preferred_element_type=f32)
    edge = edge_control[...] + result.reshape(edge_control.shape)
    for n in range(2):
        ends[0, n] = edge[n]
        ends[1, 1 - n] = edge[2 + n]
    copies.append(put(ends.at[0], pl.ds(0, 2), 1))
    copies.append(put(ends.at[1], pl.ds(rows - 2, 2), 2))
    sublane = lax.broadcasted_iota(jnp.int32, (8, width), 0)
    for side in range(2):
        start = side * (cols - 8)
        for i in range(2, rows - 2):
            block = inner[i, start : start + 8, :]
            for n in range(2):
                outer = jnp.broadcast_to(edge[4 + 2 * side + n, i : i + 1, :], (8, width))
                block = jnp.where(sublane == (n if side == 0 else 7 - n), outer, block)
            flanks[side, i - 2] = block
        copies.append(put(flanks.at[side], (body, pl.ds(start, 8)), 3 + side))
    for copy in copies:
        copy.wait()


def finish_edges(inside, center, left, right, borders, vertical_half, edge_control, inner):
    rows, cols, width = center.shape
    return pl.pallas_call(
        finish_edges_kernel,
        out_shape=jax.ShapeDtypeStruct(inner.shape, f32),
        in_specs=[SMEM] + [VMEM] * 10,
        out_specs=HBM,
        scratch_shapes=[
            pltpu.VMEM((2, 2, cols, width), f32),
            pltpu.VMEM((2, 2, around, width), f32),
            pltpu.VMEM((8 * rows, width), bf16),
            pltpu.VMEM((2, 2, cols, width), f32),
            pltpu.VMEM((2, rows - 4, 8, width), f32),
            pltpu.SemaphoreType.DMA((5,)),
        ],
        cost_estimate=pl.CostEstimate(
            flops=16 * rows * width * width, bytes_accessed=4 * rows * cols * width, transcendentals=0
        ),
        compiler_params=pltpu.CompilerParams(vmem_limit_bytes=16 * mebi),
    )(inside, center, left, right, *borders, vertical_half, edge_control, inner)


def on_device(
    control,
    vertical_half,
    error_scale,
    jacobian,
    inverse_r,
    channel_mask,
    group_instrument,
    outbound_columns,
    observation_row,
):
    rows, cols, width = control.shape
    devices = lax.axis_size("lat") * lax.axis_size("lon")
    slots = outbound_columns.size
    lists = outbound_columns.reshape(parts, 1, slots // parts)
    inside = inside_poles()

    def exchange(columns):
        return lax.all_to_all(
            columns.reshape(devices, slots // devices, width),
            ("lat", "lon"),
            split_axis=0,
            concat_axis=0,
            tiled=True,
        ).reshape(slots, width)

    own = own_borders(control)
    vertical, left, right, scale, edge_scale, edge_control = lift(control, error_scale, vertical_half)
    borders, held = exchange_borders(*own, vertical)
    inner, picker = pick_inside(held, scale, lists)
    outgoing = pick_edges(
        inside, vertical, left, right, borders, vertical_half, edge_scale, picker, inner
    )
    slot_adjoint = observe(
        exchange(outgoing), jacobian[0], inverse_r, channel_mask, group_instrument[0], observation_row
    )
    returned = exchange(slot_adjoint)
    scaled, left, right = gather(scale, lists, returned)
    borders, held = exchange_borders(*gather_edges(edge_scale, lists, returned), scaled)
    inner = finish_inside(held, vertical_half, control)
    return finish_edges(
        inside, scaled, left, right, borders, vertical_half, edge_control, inner
    )


def solution(mesh):
    placed = (
        P("lat", "lon", None),
        P(),
        P("lat", "lon", None),
        P(("lat", "lon"), None, None),
        P(),
        P(("lat", "lon"), None, None),
        P(("lat", "lon"), None),
        P(("lat", "lon"), None),
        P(("lat", "lon"), None, None),
    )
    return jax.shard_map(
        on_device, mesh=mesh, in_specs=placed, out_specs=P("lat", "lon", None), check_vma=False
    )
```
